128 devices in a mesh: img: 4 (over z_lo, core), exp: 32 (over x, y, z_hi).
Axes of the slice: x: 4, y: 4, z: 4 (z_hi: 2, z_lo: 2; z = z_hi * 2 + z_lo), core: 2. Of those that a mesh axis runs over, the one named last changes fastest.
Arguments:
- context: bfloat16 [256, 256, 1024], P(('img', 'exp')), may hold values from -1.5 to 1.5
- residual: bfloat16 [256, 256, 1024], P(('img', 'exp')), may hold values from -1.5 to 1.5
- cotangent: bfloat16 [256, 256, 1024], P(('img', 'exp')), may hold values from -6 to 6
- proj_weight: bfloat16 [1024, 1024], P('img'), may hold values from -0.1875 to 0.1875
- slot_params: bfloat16 [1024, 64], replicated, may hold values from -0.1875 to 0.1875
- expert_in: bfloat16 [64, 1024, 4096], P('exp', None, 'img'), may hold values from -0.1875 to 0.1875
- expert_out: bfloat16 [64, 4096, 1024], P('exp', 'img'), may hold values from -0.09375 to 0.09375
Outputs:
- grad_context: bfloat16 [256, 256, 1024], P(('img', 'exp'))
- grad_residual: bfloat16 [256, 256, 1024], P(('img', 'exp'))
- grad_proj: float32 [1024, 1024], P('img')
- grad_slots: float32 [1024, 64], replicated
- grad_expert_in: bfloat16 [64, 1024, 4096], P('exp', None, 'img')
- grad_expert_out: bfloat16 [64, 4096, 1024], P('exp', 'img')
The draws below stay inside these ranges and needn't reach their ends.
All inputs are finite; a program needn't handle non-finite values.
Results may differ from the reference program's by a relative error of at most 0.025.
Values may be sent and summed in bfloat16 or wider, within the bound.
A program may use at most 128 MiB of HBM per device.

```python
import math
import jax
import jax.numpy as jnp
from jax import lax

D = 1024
FF = 4096
TOK = 256
EXPERTS = 64
IMAGES = 256


def draw_context(key, part):
    folded = jax.random.fold_in(key, 7101)
    sample = jnp.clip(0.25 * jax.random.normal(folded, (IMAGES, TOK, D), jnp.float32), -1.5, 1.5)
    return sample.astype(jnp.bfloat16)


def draw_residual(key, part):
    folded = jax.random.fold_in(key, 7202)
    sample = jnp.clip(0.25 * jax.random.normal(folded, (IMAGES, TOK, D), jnp.float32), -1.5, 1.5)
    return sample.astype(jnp.bfloat16)


def levels(key, extent, shards, smallest, largest):
    level = 1.0
    for axis_at, shards_of in shards:
        heights = jax.random.uniform(jax.random.fold_in(jax.random.fold_in(key, 6), axis_at), (shards_of,), jnp.float32, smallest / len(shards), largest / len(shards))
        level = level * jnp.repeat(jnp.exp(heights), extent[axis_at] // shards_of).reshape((-1,) + (1,) * (len(extent) - 1 - axis_at))
    return level


def scatter_about(stream_key, shape, deviation, reach, split=(), held_as=jnp.bfloat16):
    gain = levels(stream_key, shape, split, -0.22, 0.18) if split else 1.0
    drawn = jax.random.normal(stream_key, shape, jnp.float32) * deviation * gain
    return jnp.minimum(jnp.maximum(drawn, -reach), reach).astype(held_as)


def setup_inputs(seed: int = 0) -> dict:
    splits = jax.random.split(jax.random.key(seed), 8)
    context = draw_context(jax.random.fold_in(splits[7], 71), 0)
    residual = draw_residual(jax.random.fold_in(splits[7], 71), 0)
    cotangent = scatter_about(splits[2], (IMAGES, TOK, D), 1.0, 6.0, ((0, 128),))
    proj_weight = scatter_about(splits[3], (D, D), D ** -0.5, 0.1875, ((0, 4),))
    slot_params = scatter_about(splits[4], (D, EXPERTS), D ** -0.5, 0.1875)
    expert_in = scatter_about(splits[5], (EXPERTS, D, FF), D ** -0.5, 0.1875, ((0, 32), (2, 4)))
    expert_out = scatter_about(splits[6], (EXPERTS, FF, D), FF ** -0.5, 0.09375, ((0, 32), (1, 4)))
    return dict(context=context, residual=residual, cotangent=cotangent, proj_weight=proj_weight, slot_params=slot_params, expert_in=expert_in, expert_out=expert_out)


logit_scale = 48.0
epsilon = 1e-06

def gelu_back(pre, upstream):
    return jax.vjp(jax.nn.gelu, pre)[1](upstream)[0]

def reference(context, residual, cotangent, proj_weight, slot_params, expert_in, expert_out):
    width = context.shape[2]
    images, tokens = (context.shape[0], context.shape[1])
    factor = logit_scale / math.sqrt(width)
    flat_ctx = context.reshape(images * tokens, width)
    stream = (residual.reshape(-1, width).astype(jnp.float32) + jnp.dot(flat_ctx, proj_weight, preferred_element_type=jnp.float32)).astype(jnp.bfloat16)
    stream32 = stream.astype(jnp.float32)
    inverse = lax.rsqrt(lax.optimization_barrier(jnp.mean(stream32 * stream32, axis=-1, keepdims=True)) + epsilon)
    normed32 = stream32 * inverse
    normed = normed32.astype(jnp.bfloat16)
    params32 = slot_params.astype(jnp.float32)
    slot_norm = jnp.sqrt(lax.optimization_barrier(jnp.sum(params32 * params32, axis=0, keepdims=True)) + epsilon)
    unit32 = params32 / slot_norm
    unit = unit32.astype(jnp.bfloat16)
    logits = factor * jnp.dot(normed, unit, preferred_element_type=jnp.float32)
    logits = logits.reshape(images, tokens, -1)
    expo = jnp.exp(logits)
    dispatch32 = expo / lax.optimization_barrier(jnp.sum(expo, axis=1, keepdims=True))
    combine32 = expo / lax.optimization_barrier(jnp.sum(expo, axis=2, keepdims=True))
    dispatch = dispatch32.astype(jnp.bfloat16)
    combine = combine32.astype(jnp.bfloat16)
    normed3 = normed.reshape(images, tokens, width)
    slot_in = jnp.einsum('bms,bmd->bsd', dispatch.astype(jnp.float32), normed3.astype(jnp.float32)).astype(jnp.bfloat16)
    slot_major = jnp.transpose(slot_in, (1, 0, 2))

    def forward_one(items):
        rows, first, second = items
        pre = jnp.dot(rows, first, preferred_element_type=jnp.float32)
        act = jax.nn.gelu(pre).astype(jnp.bfloat16)
        return jnp.dot(act, second, preferred_element_type=jnp.float32).astype(jnp.bfloat16)
    slot_out = jnp.transpose(lax.map(forward_one, (slot_major, expert_in, expert_out)), (1, 0, 2))
    upstream3 = cotangent.astype(jnp.float32)
    grad_slot_out = jnp.einsum('bms,bmd->bsd', combine.astype(jnp.float32), upstream3).astype(jnp.bfloat16)
    grad_combine = jnp.einsum('bmd,bsd->bms', upstream3, slot_out.astype(jnp.float32))
    grad_major = jnp.transpose(grad_slot_out, (1, 0, 2))

    def backward_one(items):
        rows, first, second, grads = items
        pre = jnp.dot(rows, first, preferred_element_type=jnp.float32)
        act = jax.nn.gelu(pre).astype(jnp.bfloat16)
        grad_act = jnp.dot(grads, second.T, preferred_element_type=jnp.float32)
        grad_pre = gelu_back(pre, grad_act).astype(jnp.bfloat16)
        grad_second = jnp.dot(act.T, grads, preferred_element_type=jnp.float32).astype(jnp.bfloat16)
        grad_first = jnp.dot(rows.T, grad_pre, preferred_element_type=jnp.float32).astype(jnp.bfloat16)
        grad_rows = jnp.dot(grad_pre, first.T, preferred_element_type=jnp.float32).astype(jnp.bfloat16)
        return (grad_first, grad_second, grad_rows)
    grad_expert_in, grad_expert_out, grad_rows = lax.map(backward_one, (slot_major, expert_in, expert_out, grad_major))
    grad_slot_in = jnp.transpose(grad_rows, (1, 0, 2))
    grad_dispatch = jnp.einsum('bmd,bsd->bms', normed3.astype(jnp.float32), grad_slot_in.astype(jnp.float32))
    grad_logits32 = combine32 * (grad_combine - lax.optimization_barrier(jnp.sum(combine32 * grad_combine, axis=2, keepdims=True)))
    grad_logits32 = grad_logits32 + dispatch32 * (grad_dispatch - lax.optimization_barrier(jnp.sum(dispatch32 * grad_dispatch, axis=1, keepdims=True)))
    grad_logits = grad_logits32.astype(jnp.bfloat16).reshape(images * tokens, -1)
    grad_normed = jnp.einsum('bms,bsd->bmd', dispatch.astype(jnp.float32), grad_slot_in.astype(jnp.float32)).reshape(images * tokens, width)
    grad_normed = grad_normed + factor * jnp.dot(grad_logits, unit.T, preferred_element_type=jnp.float32)
    grad_unit = factor * jnp.dot(normed.T, grad_logits, preferred_element_type=jnp.float32)
    grad_slots = (grad_unit - unit32 * lax.optimization_barrier(jnp.sum(unit32 * grad_unit, axis=0, keepdims=True))) / slot_norm
    upstream = cotangent.reshape(-1, width).astype(jnp.float32)
    grad_stream = upstream + inverse * (grad_normed - normed32 * lax.optimization_barrier(jnp.mean(normed32 * grad_normed, axis=-1, keepdims=True)))
    grad_residual = grad_stream.astype(jnp.bfloat16)
    grad_context = jnp.dot(grad_residual, proj_weight.T, preferred_element_type=jnp.float32).astype(jnp.bfloat16)
    grad_proj = jnp.dot(flat_ctx.T, grad_residual, preferred_element_type=jnp.float32)
    return (grad_context.reshape(images, tokens, width), grad_residual.reshape(images, tokens, width), grad_proj, grad_slots, grad_expert_in, grad_expert_out)
```

```python
import math

import jax
import jax.numpy as jnp
from jax import lax
from jax.experimental import pallas as pl
from jax.experimental.pallas import tpu as pltpu
from jax.sharding import Mesh
from jax.sharding import PartitionSpec as P

AXES = ("zl", "core", "x", "y", "zh")
IMG = ("zl", "core")
EXP = ("x", "y", "zh")
IMG_EXP = IMG + EXP
MESH = pl.DeviceIdType.MESH
VMEM = pltpu.VMEM
BF16 = jnp.bfloat16
F32 = jnp.float32


logit_scale = 48.0
epsilon = 1e-06


def place():
    zl, core, x, y, zh = (lax.axis_index(a) for a in AXES)
    return 2 * zh + zl, core, 4 * x + y


def flip(bit):
    return 1 - bit


def mate(z):
    return z + 1 - 2 * lax.rem(z, 2)


def cross(z):
    return 3 - z


def far(z):
    return lax.rem(z + 2, 4)


def at_z(z):
    return {"zl": lax.rem(z, 2), "zh": lax.div(z, 2)}


def at_core(core):
    return {"core": core}


def at_xy(k):
    return {"x": lax.div(k, 4), "y": lax.rem(k, 4)}


def remote(src, dst, send, recv, device):
    return pltpu.make_async_remote_copy(
        src_ref=src, dst_ref=dst, send_sem=send, recv_sem=recv, device_id=device, device_id_type=MESH
    )


def greet(devices, xy=None):
    barrier = pltpu.get_barrier_semaphore()
    for device in devices:
        pl.semaphore_signal(barrier, inc=1, device_id=device, device_id_type=MESH)
    count = len(devices)
    if xy is not None:

        def one(d, carry):
            pl.semaphore_signal(
                barrier, inc=1, device_id=at_xy(lax.rem(xy + d, 16)), device_id_type=MESH
            )
            return carry

        lax.fori_loop(1, 16, one, 0)
        count += 15
    pl.semaphore_wait(barrier, count)


def xy_copy(d, xy, src, dst, send, recv):
    k = lax.rem(xy + d, 16)
    return remote(src(k), dst(xy), send.at[d], recv.at[d], at_xy(k))


def xy_start(*args):
    def one(d, carry):
        xy_copy(d, *args).start()
        return carry

    lax.fori_loop(1, 16, one, 0)


def xy_wait(*args):
    def one(d, carry):
        xy_copy(d, *args).wait()
        return carry

    lax.fori_loop(1, 16, one, 0)


def rows8(ref, kind, k):
    return ref.at[kind, pl.ds(pl.multiple_of(8 * k, 8), 8)]


def one_hot(wanted):
    rows = lax.broadcasted_iota(jnp.int32, (128, 128), 0)
    columns = lax.broadcasted_iota(jnp.int32, (128, 128), 1)
    return (columns == wanted(rows)).astype(F32).astype(BF16)


def bits(value, low, count):
    return lax.rem(lax.div(value, 2**low), 2**count)


def to_pairs(r):
    return bits(r, 0, 1) * 64 + bits(r, 1, 6)


def from_pairs(r):
    return bits(r, 0, 6) * 2 + bits(r, 6, 1)


def to_blocks(r):
    return bits(r, 1, 4) * 8 + bits(r, 6, 1) * 4 + bits(r, 5, 1) * 2 + bits(r, 0, 1)


def from_blocks(r):
    return bits(r, 2, 1) * 64 + bits(r, 1, 1) * 32 + bits(r, 3, 4) * 2 + bits(r, 0, 1)


def reorder(wanted, rows):
    return jnp.dot(one_hot(wanted), rows, preferred_element_type=F32).astype(BF16)


def params(number, limit=None):
    return pltpu.CompilerParams(
        collective_id=number, has_side_effects=True, vmem_limit_bytes=limit or (40 << 20)
    )


def weight_kernel(own, out, s_sem, r_sem):
    z, core, _ = place()
    block = 2 * lax.rem(z, 2) + core
    other = 2 * flip(lax.rem(z, 2)) + core
    half = own.shape[0] // 2

    def rows(blk, start, size):
        return out.at[pl.ds(pl.multiple_of(blk * 2 * half + start, half), size)]

    partner = at_core(flip(core))
    greet([at_z(mate(z)), at_z(cross(z)), partner])
    to_mate = remote(own.at[pl.ds(0, half)], rows(block, 0, half), s_sem.at[0], r_sem.at[0], at_z(mate(z)))
    to_cross = remote(
        own.at[pl.ds(half, half)], rows(block, half, half), s_sem.at[1], r_sem.at[1], at_z(cross(z))
    )
    to_core = remote(own, rows(block, 0, 2 * half), s_sem.at[2], r_sem.at[2], partner)
    to_mate.start()
    to_cross.start()
    to_core.start()
    mine = pltpu.make_async_copy(own, rows(block, 0, 2 * half), s_sem.at[5])
    mine.start()
    first = remote(rows(other, 0, half), rows(other, 0, half), s_sem.at[3], r_sem.at[3], partner)
    second = remote(rows(other, half, half), rows(other, half, half), s_sem.at[4], r_sem.at[4], partner)
    to_mate.wait_recv()
    first.start()
    to_cross.wait_recv()
    second.start()
    mine.wait()
    to_mate.wait_send()
    to_cross.wait_send()
    to_core.wait()
    first.wait()
    second.wait()


def whole_weight(own):
    rows, width = own.shape
    return pl.pallas_call(
        weight_kernel,
        out_shape=jax.ShapeDtypeStruct((4 * rows, width), own.dtype),
        in_specs=[pl.BlockSpec(memory_space=VMEM)],
        out_specs=pl.BlockSpec(memory_space=VMEM),
        scratch_shapes=[pltpu.SemaphoreType.DMA((6,)), pltpu.SemaphoreType.DMA((5,))],
        compiler_params=params(1),
        name="whole_weight",
    )(own)


def out_kernel(a_ref, b_ref, x_ref, pairs, came, blocks, s1, r1, s2, r2):
    z, core, xy = place()
    zh = lax.div(z, 2)
    partner = at_core(flip(core))
    greet([at_z(mate(z)), at_z(cross(z)), partner], xy)

    def swap(kind):
        return (
            xy,
            lambda k: rows8(pairs, kind, k),
            lambda k: rows8(came, kind, k),
            s1.at[kind],
            r1.at[kind],
        )

    def keep(kind):
        return pltpu.make_async_copy(
            rows8(pairs, kind, xy), rows8(came, kind, xy), s1.at[kind, 0]
        )

    for kind, ref in enumerate((a_ref, b_ref)):
        pairs[kind] = reorder(to_pairs, ref[...])
        keep(kind).start()
        xy_start(*swap(kind))

    def there(kind, zz):
        return x_ref.at[kind, :, zz, core]

    def send(kind, number, src, zz, device):
        return remote(src, there(kind, zz), s2.at[kind, number], r2.at[kind, number], device)

    def firsts(kind):
        return (
            send(kind, 0, blocks.at[kind, zh], z, at_z(mate(z))),
            send(kind, 1, blocks.at[kind, flip(zh)], z, at_z(cross(z))),
            send(kind, 3, blocks.at[kind, zh], z, partner),
        )

    def passed(kind):
        c, m, f = cross(z), mate(z), far(z)
        return (
            send(kind, 2, there(kind, c), c, at_z(m)),
            send(kind, 4, there(kind, c), c, partner),
            send(kind, 5, there(kind, m), m, partner),
            send(kind, 6, there(kind, f), f, partner),
        )

    def mine(kind):
        return pltpu.make_async_copy(blocks.at[kind, zh], there(kind, z), s2.at[kind, 7])

    for kind in range(2):
        keep(kind).wait()
        xy_wait(*swap(kind))
        ordered = reorder(to_blocks, came[kind])
        for i in range(2):
            for e in range(2):
                blocks[kind, i, e] = ordered[i * 64 + e * 32 : i * 64 + e * 32 + 32]
        for copy in firsts(kind):
            copy.start()
        mine(kind).start()
    for kind in range(2):
        to_mate, to_cross, to_core = firsts(kind)
        on_mate, on_core_c, on_core_m, on_core_f = passed(kind)
        to_cross.wait_recv()
        on_mate.start()
        on_core_c.start()
        to_mate.wait_recv()
        on_core_m.start()
        on_mate.wait_recv()
        on_core_f.start()
    for kind in range(2):
        to_mate, to_cross, to_core = firsts(kind)
        on_mate, on_core_c, on_core_m, on_core_f = passed(kind)
        mine(kind).wait()
        to_mate.wait_send()
        to_cross.wait_send()
        on_mate.wait_send()
        to_core.wait()
        on_core_c.wait()
        on_core_m.wait()
        on_core_f.wait()


def to_experts(first, second):
    width = first.shape[-1]
    return pl.pallas_call(
        out_kernel,
        out_shape=jax.ShapeDtypeStruct((2, 2, 4, 2, 32, width), BF16),
        in_specs=[pl.BlockSpec(memory_space=VMEM)] * 2,
        out_specs=pl.BlockSpec(memory_space=VMEM),
        scratch_shapes=[
            VMEM((2, 128, width), BF16),
            VMEM((2, 128, width), BF16),
            VMEM((2, 2, 2, 32, width), BF16),
            pltpu.SemaphoreType.DMA((2, 16)),
            pltpu.SemaphoreType.DMA((2, 16)),
            pltpu.SemaphoreType.DMA((2, 8)),
            pltpu.SemaphoreType.DMA((2, 8)),
        ],
        compiler_params=params(2),
        name="to_experts",
    )(first, second)


def back_kernel(
    o0, o1, out, halves, chip, paired, crossing, blocks, pairs, came, sa, ra, sb, rb, sc, rc
):
    z, core, xy = place()
    zh = lax.div(z, 2)
    partner = at_core(flip(core))
    greet([at_z(mate(z)), at_z(cross(z)), partner], xy)
    parts = (o0, o1)

    def to_core(kind):
        return remote(
            parts[kind].at[:, :, flip(core)], halves.at[kind], sa.at[kind], ra.at[kind], partner
        )

    def to_mate(kind):
        m = mate(z)
        return [
            remote(chip.at[kind, zz], paired.at[kind, i], sb.at[kind, i], rb.at[kind, i], at_z(m))
            for i, zz in enumerate((far(z), m))
        ]

    def to_cross(kind):
        return remote(
            crossing.at[kind], blocks.at[kind, zh], sb.at[kind, 2], rb.at[kind, 2], at_z(cross(z))
        )

    def swap(kind):
        return (
            xy,
            lambda k: rows8(pairs, kind, k),
            lambda k: rows8(came, kind, k),
            sc.at[kind],
            rc.at[kind],
        )

    def keep(kind):
        return pltpu.make_async_copy(
            rows8(pairs, kind, xy), rows8(came, kind, xy), sc.at[kind, 0]
        )

    for kind in range(2):
        to_core(kind).start()
    for kind in range(2):
        to_core(kind).wait()
        for e in range(2):
            for zz in range(4):
                chip[kind, zz, e] = (
                    parts[kind][e, zz, core].astype(F32) + halves[kind, e, zz].astype(F32)
                ).astype(BF16)
        for copy in to_mate(kind):
            copy.start()
    for kind in range(2):
        on, own = to_mate(kind)
        on.wait_recv()
        for e in range(2):
            crossing[kind, e] = (
                chip[kind, cross(z), e].astype(F32) + paired[kind, 0, e].astype(F32)
            ).astype(BF16)
        to_cross(kind).start()
        own.wait_recv()
        for e in range(2):
            blocks[kind, zh, e] = (
                chip[kind, z, e].astype(F32) + paired[kind, 1, e].astype(F32)
            ).astype(BF16)
    for kind in range(2):
        to_cross(kind).wait_recv()
        rows = jnp.concatenate([blocks[kind, i, e] for i in range(2) for e in range(2)], axis=0)
        pairs[kind] = reorder(from_blocks, rows)
        keep(kind).start()
        xy_start(*swap(kind))
    for kind in range(2):
        keep(kind).wait()
        xy_wait(*swap(kind))
        out[kind] = reorder(from_pairs, came[kind])
    for kind in range(2):
        for copy in to_mate(kind):
            copy.wait_send()
        to_cross(kind).wait_send()


def to_images(first, second):
    width = first.shape[-1]
    return pl.pallas_call(
        back_kernel,
        out_shape=jax.ShapeDtypeStruct((2, 128, width), BF16),
        in_specs=[pl.BlockSpec(memory_space=VMEM)] * 2,
        out_specs=pl.BlockSpec(memory_space=VMEM),
        scratch_shapes=[
            VMEM((2, 2, 4, 32, width), BF16),
            VMEM((2, 4, 2, 32, width), BF16),
            VMEM((2, 2, 2, 32, width), BF16),
            VMEM((2, 2, 32, width), BF16),
            VMEM((2, 2, 2, 32, width), BF16),
            VMEM((2, 128, width), BF16),
            VMEM((2, 128, width), BF16),
            pltpu.SemaphoreType.DMA((2,)),
            pltpu.SemaphoreType.DMA((2,)),
            pltpu.SemaphoreType.DMA((2, 3)),
            pltpu.SemaphoreType.DMA((2, 3)),
            pltpu.SemaphoreType.DMA((2, 16)),
            pltpu.SemaphoreType.DMA((2, 16)),
        ],
        compiler_params=params(3),
        name="to_images",
    )(first, second)


def sum_kernel(
    g, u, out, u_out,
    ga, gq, gb, gh, gc, gt, gf, gv, gall,
    ua, uw, uc, ut, uz, uv, uall, uother,
    sg, rg, su, ru, s1, r1, s2, r2, s3, r3, s4, r4,
):
    z, core, xy = place()
    zl = lax.rem(z, 2)
    partner = at_core(flip(core))
    ring = [at_z(lax.rem(z + d, 4)) for d in range(1, 4)]
    greet([*ring, partner], xy)
    half = g.shape[2] // 2
    width = g.shape[3]
    chunk = 2 * half // 16
    wide = width // 4

    u_core = remote(u.at[flip(core)], ua, su.at[0], ru.at[0], partner)
    g_core = remote(g.at[:, flip(core)], ga, sg.at[0], rg.at[0], partner)
    u_core.start()
    g_core.start()

    u_swap = (xy, lambda k: uw.at[k], lambda k: uc.at[k], s1, r1)
    u_keep = pltpu.make_async_copy(uw.at[xy], uc.at[xy], s1.at[0])
    u_core.wait()
    for i in range(4):
        for j in range(4):
            where = (slice(8 * i, 8 * i + 8), slice(wide * j, wide * j + wide))
            uw[4 * i + j] = u[core, where[0], where[1]] + ua[where[0], where[1]]
    u_keep.start()
    xy_start(*u_swap)

    g_core.wait()
    gq[...] = (g[flip(zl), core].astype(F32) + ga[flip(zl)].astype(F32)).astype(BF16)
    g_mate = remote(
        gq.at[pl.ds(0, half)], gb.at[pl.ds(0, half)], sg.at[1], rg.at[1], at_z(mate(z))
    )
    g_cross = remote(
        gq.at[pl.ds(half, half)], gb.at[pl.ds(half, half)], sg.at[2], rg.at[2], at_z(cross(z))
    )
    g_mate.start()
    g_cross.start()

    u_keep.wait()
    xy_wait(*u_swap)
    ut[...] = jnp.sum(uc[...], axis=0)
    u_ring = [
        remote(ut, uz.at[z], su.at[d + 1], ru.at[d + 1], ring[d]) for d in range(3)
    ]
    u_mine = pltpu.make_async_copy(ut, uz.at[z], su.at[4])
    u_mine.start()
    for copy in u_ring:
        copy.start()

    g_mate.wait()
    g_cross.wait()
    gh[...] = (
        g[zl, core].astype(F32) + ga[zl].astype(F32) + gb[...].astype(F32)
    ).astype(BF16)
    g_swap = (
        xy,
        lambda k: gh.at[pl.ds(pl.multiple_of(chunk * k, chunk), chunk)],
        lambda k: gc.at[k],
        s2,
        r2,
    )
    g_keep = pltpu.make_async_copy(g_swap[1](xy), gc.at[xy], s2.at[0])
    g_keep.start()
    xy_start(*g_swap)

    u_mine.wait()
    for copy in u_ring:
        copy.wait()
    uv[...] = jnp.sum(uz[...], axis=0)
    u_back = (xy, lambda k: uv, lambda k: uall.at[k], s3, r3)
    u_stay = pltpu.make_async_copy(uv, uall.at[xy], s3.at[0])
    u_stay.start()
    xy_start(*u_back)

    g_keep.wait()
    xy_wait(*g_swap)
    total = gc[0].astype(F32)
    for k in range(1, 16):
        total = total + gc[k].astype(F32)
    gt[...] = total.astype(BF16)
    g_far = remote(gt, gf, sg.at[3], rg.at[3], at_z(far(z)))
    g_far.start()

    u_stay.wait()
    xy_wait(*u_back)
    u_other = remote(uall, uother, su.at[5], ru.at[5], partner)
    u_other.start()

    g_far.wait()
    gv[...] = (gt[...].astype(F32) + gf[...].astype(F32)).astype(BF16)
    g_back = (xy, lambda k: gv, lambda k: gall.at[k], s4, r4)
    g_stay = pltpu.make_async_copy(gv, gall.at[xy], s4.at[0])
    g_stay.start()
    xy_start(*g_back)

    u_other.wait()
    for i in range(4):
        for j in range(4):
            columns = slice(wide * j, wide * j + wide)
            rows = slice(8 * i, 8 * i + 8)
            u_out[core, rows, columns] = uall[4 * i + j]
            u_out[flip(core), rows, columns] = uother[4 * i + j]
    g_stay.wait()
    xy_wait(*g_back)
    for k in range(16):
        out[chunk * k : chunk * k + chunk] = gall[k].astype(F32)


def sums(partial, unit_partial):
    width = partial.shape[-1]
    rows = partial.shape[0] // 4
    chunk = rows // 16
    wide = width // 4
    dma = pltpu.SemaphoreType.DMA
    return pl.pallas_call(
        sum_kernel,
        out_shape=(
            jax.ShapeDtypeStruct((rows, width), F32),
            jax.ShapeDtypeStruct((2, 32, width), F32),
        ),
        in_specs=[pl.BlockSpec(memory_space=VMEM)] * 2,
        out_specs=(pl.BlockSpec(memory_space=VMEM), pl.BlockSpec(memory_space=VMEM)),
        scratch_shapes=[
            VMEM((2, rows, width), BF16),
            VMEM((rows, width), BF16),
            VMEM((rows, width), BF16),
            VMEM((rows, width), BF16),
            VMEM((16, chunk, width), BF16),
            VMEM((chunk, width), BF16),
            VMEM((chunk, width), BF16),
            VMEM((chunk, width), BF16),
            VMEM((16, chunk, width), BF16),
            VMEM((32, width), F32),
            VMEM((16, 8, wide), F32),
            VMEM((16, 8, wide), F32),
            VMEM((8, wide), F32),
            VMEM((4, 8, wide), F32),
            VMEM((8, wide), F32),
            VMEM((16, 8, wide), F32),
            VMEM((16, 8, wide), F32),
            dma((4,)),
            dma((4,)),
            dma((6,)),
            dma((6,)),
            *[dma((16,))] * 8,
        ],
        compiler_params=params(4),
        name="sums",
    )(partial.reshape(2, 2, rows, width), unit_partial.reshape(2, 32, width))


def gelu_back(pre, upstream):
    return jax.vjp(jax.nn.gelu, pre)[1](upstream)[0]


def shards(context, residual, cotangent, proj_weight, slot_params, expert_in, expert_out):
    images, tokens, width = context.shape
    rows = images * tokens
    slots = slot_params.shape[1]
    factor = logit_scale / math.sqrt(width)
    flat_ctx = context.reshape(rows, width)
    weight = whole_weight(proj_weight)
    mixed = jnp.dot(flat_ctx, weight, preferred_element_type=jnp.float32)
    stream = (residual.reshape(rows, width).astype(jnp.float32) + mixed).astype(jnp.bfloat16)
    stream32 = stream.astype(jnp.float32)
    inverse = lax.rsqrt(jnp.mean(stream32 * stream32, axis=-1, keepdims=True) + epsilon)
    normed32 = stream32 * inverse
    normed = normed32.astype(jnp.bfloat16)
    params32 = slot_params.astype(jnp.float32)
    slot_norm = jnp.sqrt(jnp.sum(params32 * params32, axis=0, keepdims=True) + epsilon)
    unit32 = params32 / slot_norm
    unit = unit32.astype(jnp.bfloat16)
    logits = factor * jnp.dot(normed, unit, preferred_element_type=jnp.float32)
    logits = logits.reshape(images, tokens, -1)
    expo = jnp.exp(logits)
    dispatch32 = expo / jnp.sum(expo, axis=1, keepdims=True)
    combine32 = expo / jnp.sum(expo, axis=2, keepdims=True)
    dispatch = dispatch32.astype(jnp.bfloat16)
    combine = combine32.astype(jnp.bfloat16)
    normed3 = normed.reshape(images, tokens, width)
    slot_in = jnp.einsum(
        "bms,bmd->bsd", dispatch, normed3, preferred_element_type=jnp.float32
    ).astype(jnp.bfloat16)
    grad_slot_out = jnp.einsum(
        "bms,bmd->bsd", combine, cotangent, preferred_element_type=jnp.float32
    ).astype(jnp.bfloat16)
    arrived = to_experts(
        slot_in.reshape(images * slots, width), grad_slot_out.reshape(images * slots, width)
    ).reshape(2, 2, 256, width)
    slot_rows, grad_rows = arrived[0], arrived[1]
    pre = jnp.einsum("jgd,jdf->jgf", slot_rows, expert_in, preferred_element_type=jnp.float32)
    act = jax.nn.gelu(pre).astype(jnp.bfloat16)
    out_part = jnp.einsum(
        "jgf,jfd->jgd", act, expert_out, preferred_element_type=jnp.float32
    ).astype(jnp.bfloat16)
    grad_act = jnp.einsum(
        "jgd,jfd->jgf", grad_rows, expert_out, preferred_element_type=jnp.float32
    )
    grad_pre = gelu_back(pre, grad_act).astype(jnp.bfloat16)
    grad_part = jnp.einsum(
        "jgf,jdf->jgd", grad_pre, expert_in, preferred_element_type=jnp.float32
    ).astype(jnp.bfloat16)
    returned = to_images(
        out_part.reshape(2, 4, 2, 32, width), grad_part.reshape(2, 4, 2, 32, width)
    ).reshape(2, images, slots, width)
    slot_out, grad_slot_in = returned[0], returned[1]
    grad_expert_out = jnp.einsum(
        "jgf,jgd->jfd", act, grad_rows, preferred_element_type=jnp.float32
    ).astype(jnp.bfloat16)
    grad_expert_in = jnp.einsum(
        "jgd,jgf->jdf", slot_rows, grad_pre, preferred_element_type=jnp.float32
    ).astype(jnp.bfloat16)
    grad_combine = jnp.einsum(
        "bmd,bsd->bms", cotangent, slot_out, preferred_element_type=jnp.float32
    )
    grad_dispatch = jnp.einsum(
        "bmd,bsd->bms", normed3, grad_slot_in, preferred_element_type=jnp.float32
    )
    grad_logits32 = combine32 * (
        grad_combine - jnp.sum(combine32 * grad_combine, axis=2, keepdims=True)
    )
    grad_logits32 = grad_logits32 + dispatch32 * (
        grad_dispatch - jnp.sum(dispatch32 * grad_dispatch, axis=1, keepdims=True)
    )
    grad_logits = grad_logits32.astype(jnp.bfloat16).reshape(rows, -1)
    grad_normed = jnp.einsum(
        "bms,bsd->bmd", dispatch, grad_slot_in, preferred_element_type=jnp.float32
    ).reshape(rows, width)
    grad_normed = grad_normed + factor * jnp.dot(
        grad_logits, unit.T, preferred_element_type=jnp.float32
    )
    local_unit = jnp.dot(grad_logits.T, normed, preferred_element_type=jnp.float32)
    upstream = cotangent.reshape(rows, width).astype(jnp.float32)
    grad_stream = upstream + inverse * (
        grad_normed - normed32 * jnp.mean(normed32 * grad_normed, axis=-1, keepdims=True)
    )
    grad_residual = grad_stream.astype(jnp.bfloat16)
    grad_context = jnp.dot(
        grad_residual, weight.T, preferred_element_type=jnp.float32
    ).astype(jnp.bfloat16)
    partial = jnp.dot(
        flat_ctx.T, grad_residual, preferred_element_type=jnp.float32
    ).astype(jnp.bfloat16)
    grad_proj, unit_sum = sums(partial, local_unit)
    grad_unit = factor * unit_sum.reshape(slots, width).T
    grad_slots = (
        grad_unit - unit32 * jnp.sum(unit32 * grad_unit, axis=0, keepdims=True)
    ) / slot_norm
    return (
        grad_context.reshape(images, tokens, width),
        grad_residual.reshape(images, tokens, width),
        grad_proj,
        grad_slots,
        grad_expert_in,
        grad_expert_out,
    )


def solution(mesh):
    torus = Mesh(mesh.devices.reshape(2, 2, 4, 4, 2), AXES)
    placed = (
        P(IMG_EXP, None, None),
        P(IMG_EXP, None, None),
        P(IMG_EXP, None, None),
        P(IMG, None),
        P(),
        P(EXP, None, IMG),
        P(EXP, IMG, None),
    )
    return jax.shard_map(
        shards,
        mesh=torus,
        in_specs=placed,
        out_specs=(
            P(IMG_EXP, None, None),
            P(IMG_EXP, None, None),
            P(IMG, None),
            P(),
            P(EXP, None, IMG),
            P(EXP, IMG, None),
        ),
        check_vma=False,
    )
```

```python
import math

import jax
import jax.numpy as jnp
from jax import lax
from jax.experimental import pallas as pl
from jax.experimental.pallas import tpu as pltpu
from jax.sharding import Mesh
from jax.sharding import PartitionSpec as P

AXES = ("zl", "core", "x", "y", "zh")
IMG = ("zl", "core")
EXP = ("x", "y", "zh")
IMG_EXP = IMG + EXP
MESH = pl.DeviceIdType.MESH
VMEM = pltpu.VMEM
BF16 = jnp.bfloat16
F32 = jnp.float32


logit_scale = 48.0
epsilon = 1e-06


def place():
    zl, core, x, y, zh = (lax.axis_index(a) for a in AXES)
    return 2 * zh + zl, core, 4 * x + y


def flip(bit):
    return 1 - bit


def mate(z):
    return z + 1 - 2 * lax.rem(z, 2)


def cross(z):
    return 3 - z


def far(z):
    return lax.rem(z + 2, 4)


def at_z(z):
    return {"zl": lax.rem(z, 2), "zh": lax.div(z, 2)}


def at_core(core):
    return {"core": core}


def at_xy(k):
    return {"x": lax.div(k, 4), "y": lax.rem(k, 4)}


def remote(src, dst, send, recv, device):
    return pltpu.make_async_remote_copy(
        src_ref=src, dst_ref=dst, send_sem=send, recv_sem=recv, device_id=device, device_id_type=MESH
    )


def greet(devices, xy=None):
    barrier = pltpu.get_barrier_semaphore()
    for device in devices:
        pl.semaphore_signal(barrier, inc=1, device_id=device, device_id_type=MESH)
    count = len(devices)
    if xy is not None:

        def one(d, carry):
            pl.semaphore_signal(
                barrier, inc=1, device_id=at_xy(lax.rem(xy + d, 16)), device_id_type=MESH
            )
            return carry

        lax.fori_loop(1, 16, one, 0)
        count += 15
    pl.semaphore_wait(barrier, count)


def xy_copy(d, xy, src, dst, send, recv):
    k = lax.rem(xy + d, 16)
    return remote(src(k), dst(xy), send.at[d], recv.at[d], at_xy(k))


def xy_start(*args):
    def one(d, carry):
        xy_copy(d, *args).start()
        return carry

    lax.fori_loop(1, 16, one, 0)


def xy_wait(*args):
    def one(d, carry):
        xy_copy(d, *args).wait()
        return carry

    lax.fori_loop(1, 16, one, 0)


def rows8(ref, kind, k):
    return ref.at[kind, pl.ds(pl.multiple_of(8 * k, 8), 8)]


def one_hot(wanted):
    rows = lax.broadcasted_iota(jnp.int32, (128, 128), 0)
    columns = lax.broadcasted_iota(jnp.int32, (128, 128), 1)
    return (columns == wanted(rows)).astype(F32).astype(BF16)


def bits(value, low, count):
    return lax.rem(lax.div(value, 2**low), 2**count)


def to_pairs(r):
    return bits(r, 0, 1) * 64 + bits(r, 1, 6)


def from_pairs(r):
    return bits(r, 0, 6) * 2 + bits(r, 6, 1)


def to_blocks(r):
    return bits(r, 1, 4) * 8 + bits(r, 6, 1) * 4 + bits(r, 5, 1) * 2 + bits(r, 0, 1)


def from_blocks(r):
    return bits(r, 2, 1) * 64 + bits(r, 1, 1) * 32 + bits(r, 3, 4) * 2 + bits(r, 0, 1)


def reorder(wanted, rows):
    return jnp.dot(one_hot(wanted), rows, preferred_element_type=F32).astype(BF16)


def params(number, limit=None):
    return pltpu.CompilerParams(
        collective_id=number, has_side_effects=True, vmem_limit_bytes=limit or (40 << 20)
    )


def weight_kernel(own, out, s_sem, r_sem):
    z, core, _ = place()
    block = 2 * lax.rem(z, 2) + core
    other = 2 * flip(lax.rem(z, 2)) + core
    half = own.shape[0] // 2

    def rows(blk, start, size):
        return out.at[pl.ds(pl.multiple_of(blk * 2 * half + start, half), size)]

    partner = at_core(flip(core))
    greet([at_z(mate(z)), at_z(cross(z)), partner])
    to_mate = remote(own.at[pl.ds(0, half)], rows(block, 0, half), s_sem.at[0], r_sem.at[0], at_z(mate(z)))
    to_cross = remote(
        own.at[pl.ds(half, half)], rows(block, half, half), s_sem.at[1], r_sem.at[1], at_z(cross(z))
    )
    to_core = remote(own, rows(block, 0, 2 * half), s_sem.at[2], r_sem.at[2], partner)
    to_mate.start()
    to_cross.start()
    to_core.start()
    mine = pltpu.make_async_copy(own, rows(block, 0, 2 * half), s_sem.at[5])
    mine.start()
    first = remote(rows(other, 0, half), rows(other, 0, half), s_sem.at[3], r_sem.at[3], partner)
    second = remote(rows(other, half, half), rows(other, half, half), s_sem.at[4], r_sem.at[4], partner)
    to_mate.wait_recv()
    first.start()
    to_cross.wait_recv()
    second.start()
    mine.wait()
    to_mate.wait_send()
    to_cross.wait_send()
    to_core.wait()
    first.wait()
    second.wait()


def whole_weight(own):
    rows, width = own.shape
    return pl.pallas_call(
        weight_kernel,
        out_shape=jax.ShapeDtypeStruct((4 * rows, width), own.dtype),
        in_specs=[pl.BlockSpec(memory_space=VMEM)],
        out_specs=pl.BlockSpec(memory_space=VMEM),
        scratch_shapes=[pltpu.SemaphoreType.DMA((6,)), pltpu.SemaphoreType.DMA((5,))],
        compiler_params=params(1),
        name="whole_weight",
    )(own)


def curve(x):
    slope = math.sqrt(2 / math.pi)
    square = x * x
    t = jnp.tanh(slope * (x + 0.044715 * (square * x)))
    cdf = 0.5 * (1.0 + t)
    return x * cdf, cdf + x * (0.5 * (1.0 - t * t)) * (slope * (1.0 + 3 * 0.044715 * square))


def times(a, b):
    return jnp.dot(a, b, preferred_element_type=F32)


def times_t(a, b):
    return lax.dot_general(a, b, (((1,), (1,)), ((), ())), preferred_element_type=F32)


def t_times(a, b):
    return lax.dot_general(a, b, (((0,), (0,)), ((), ())), preferred_element_type=F32)


def expert_kernel(
    a_ref, b_ref, win, wout,
    out, gin, gout,
    pairs, came, blocks, x, wi, wo, act, slope, gpre, o,
    halves, chip, paired, crossing, blocks2, pairs2, came2, gi, go,
    s1, r1, s2, r2, sa, ra, sb, rb, sc, rc, sw, sg,
):
    z, core, xy = place()
    zh = lax.div(z, 2)
    partner = at_core(flip(core))
    width = x.shape[-1]
    hidden = act.shape[-1]
    load_in = pltpu.make_async_copy(win, wi, sw.at[0])
    load_out = pltpu.make_async_copy(wout, wo, sw.at[1])
    load_in.start()
    load_out.start()

    for kind, ref in enumerate((a_ref, b_ref)):
        pairs[kind] = reorder(to_pairs, ref[...])
    greet([at_z(mate(z)), at_z(cross(z)), partner], xy)

    def swap(kind):
        return (
            xy,
            lambda k: rows8(pairs, kind, k),
            lambda k: rows8(came, kind, k),
            s1.at[kind],
            r1.at[kind],
        )

    def keep(kind):
        return pltpu.make_async_copy(
            rows8(pairs, kind, xy), rows8(came, kind, xy), s1.at[kind, 0]
        )

    for kind in range(2):
        keep(kind).start()
        xy_start(*swap(kind))

    def there(kind, zz):
        return x.at[kind, :, zz, core]

    def send(kind, number, src, zz, device):
        return remote(src, there(kind, zz), s2.at[kind, number], r2.at[kind, number], device)

    c, m, f = cross(z), mate(z), far(z)

    def to_mate(kind):
        return send(kind, 0, blocks.at[kind, zh], z, at_z(m))

    def to_cross(kind):
        return send(kind, 1, blocks.at[kind, flip(zh)], z, at_z(c))

    def on_mate(kind):
        return send(kind, 2, there(kind, c), c, at_z(m))

    def to_core(kind, number):
        if number == 3:
            return send(kind, 3, blocks.at[kind, zh], z, partner)
        zz = (c, m, f)[number - 4]
        return send(kind, number, there(kind, zz), zz, partner)

    def mine(kind):
        return pltpu.make_async_copy(blocks.at[kind, zh], there(kind, z), s2.at[kind, 7])

    def spread(kind):
        keep(kind).wait()
        xy_wait(*swap(kind))
        ordered = reorder(to_blocks, came[kind])
        for i in range(2):
            for e in range(2):
                blocks[kind, i, e] = ordered[i * 64 + e * 32 : i * 64 + e * 32 + 32]
        to_cross(kind).start()
        to_mate(kind).start()
        to_core(kind, 3).start()
        mine(kind).start()

    def relay(kind):
        to_cross(kind).wait_recv()
        on_mate(kind).start()
        to_core(kind, 4).start()
        to_mate(kind).wait_recv()
        to_core(kind, 5).start()

    def relay_last(kind):
        on_mate(kind).wait_recv()
        to_core(kind, 6).start()

    def arrived(kind):
        mine(kind).wait()
        for number in range(3, 7):
            to_core(kind, number).wait_recv()

    def sent(kind):
        to_mate(kind).wait_send()
        to_cross(kind).wait_send()
        on_mate(kind).wait_send()
        for number in range(3, 7):
            to_core(kind, number).wait_send()

    spread(0)
    spread(1)
    relay(0)
    relay(1)
    relay_last(0)
    arrived(0)
    load_in.wait()
    load_out.wait()

    def rows_of(kind, e):
        return x[kind, e].reshape(256, width)

    cut = 512

    def up(e):
        rows = rows_of(0, e)
        for n in range(0, hidden, cut):
            value, rise = curve(times(rows, wi[e, :, n : n + cut]))
            act[e, :, n : n + cut] = value.astype(BF16)
            slope[e, :, n : n + cut] = rise

    def down(e):
        rows = act[e]
        for n in range(0, width, cut):
            part = times(rows, wo[e, :, n : n + cut]).astype(BF16)
            o[0, e, :, :, :, n : n + cut] = part.reshape(4, 2, 32, cut)

    def back_down(e):
        rows = rows_of(1, e)
        for n in range(0, hidden, cut):
            rise = times_t(rows, wo[e, n : n + cut, :])
            gpre[e, :, n : n + cut] = (rise * slope[e, :, n : n + cut]).astype(BF16)

    def back_up(e):
        rows = gpre[e]
        for n in range(0, width, cut):
            part = times_t(rows, wi[e, n : n + cut, :]).astype(BF16)
            o[1, e, :, :, :, n : n + cut] = part.reshape(4, 2, 32, cut)

    def home_core(kind, e):
        return remote(
            o.at[kind, e, :, flip(core)], halves.at[kind, e], sa.at[kind, e], ra.at[kind, e], partner
        )

    def home_mate(kind):
        return [
            remote(chip.at[kind, zz], paired.at[kind, i], sb.at[kind, i], rb.at[kind, i], at_z(m))
            for i, zz in enumerate((f, m))
        ]

    def home_cross(kind):
        return remote(
            crossing.at[kind], blocks2.at[kind, zh], sb.at[kind, 2], rb.at[kind, 2], at_z(c)
        )

    def home_swap(kind):
        return (
            xy,
            lambda k: rows8(pairs2, kind, k),
            lambda k: rows8(came2, kind, k),
            sc.at[kind],
            rc.at[kind],
        )

    def home_keep(kind):
        return pltpu.make_async_copy(
            rows8(pairs2, kind, xy), rows8(came2, kind, xy), sc.at[kind, 0]
        )

    def chip_sum(kind):
        for e in range(2):
            home_core(kind, e).wait()
            for zz in range(4):
                chip[kind, zz, e] = (
                    o[kind, e, zz, core].astype(F32) + halves[kind, e, zz].astype(F32)
                ).astype(BF16)
        for copy in home_mate(kind):
            copy.start()

    def pair_sum(kind):
        on, own = home_mate(kind)
        on.wait_recv()
        for e in range(2):
            crossing[kind, e] = (
                chip[kind, c, e].astype(F32) + paired[kind, 0, e].astype(F32)
            ).astype(BF16)
        home_cross(kind).start()
        own.wait_recv()
        for e in range(2):
            blocks2[kind, zh, e] = (
                chip[kind, z, e].astype(F32) + paired[kind, 1, e].astype(F32)
            ).astype(BF16)

    def home(kind):
        home_cross(kind).wait_recv()
        rows = jnp.concatenate([blocks2[kind, i, e] for i in range(2) for e in range(2)], axis=0)
        pairs2[kind] = reorder(from_blocks, rows)
        home_keep(kind).start()
        xy_start(*home_swap(kind))

    def landed(kind):
        home_keep(kind).wait()
        xy_wait(*home_swap(kind))
        out[kind] = reorder(from_pairs, came2[kind])

    def out_gradient(e):
        right = rows_of(1, e)
        for n in range(0, hidden, cut):
            go[e, n : n + cut, :] = t_times(act[e, :, n : n + cut], right).astype(BF16)
        pltpu.make_async_copy(go.at[e], gout.at[e], sg.at[0, e]).start()

    def in_gradient(e):
        left = rows_of(0, e)
        right = gpre[e]
        for n in range(0, width, cut):
            gi[e, n : n + cut, :] = t_times(left[:, n : n + cut], right).astype(BF16)
        pltpu.make_async_copy(gi.at[e], gin.at[e], sg.at[1, e]).start()

    up(0)
    up(1)
    relay_last(1)
    for e in range(2):
        down(e)
        home_core(0, e).start()
    arrived(1)
    back_down(0)
    back_down(1)
    chip_sum(0)
    for e in range(2):
        back_up(e)
        home_core(1, e).start()
    out_gradient(0)
    chip_sum(1)
    pair_sum(0)
    out_gradient(1)
    pair_sum(1)
    home(0)
    in_gradient(0)
    home(1)
    in_gradient(1)
    landed(0)
    landed(1)
    for kind in range(2):
        sent(kind)
        for copy in home_mate(kind):
            copy.wait_send()
        home_cross(kind).wait_send()
    for e in range(2):
        pltpu.make_async_copy(go.at[e], gout.at[e], sg.at[0, e]).wait()
        pltpu.make_async_copy(gi.at[e], gin.at[e], sg.at[1, e]).wait()


def experts(first, second, expert_in, expert_out):
    width = first.shape[-1]
    hidden = expert_in.shape[-1]
    dma = pltpu.SemaphoreType.DMA
    return pl.pallas_call(
        expert_kernel,
        out_shape=(
            jax.ShapeDtypeStruct((2, 128, width), BF16),
            jax.ShapeDtypeStruct(expert_in.shape, BF16),
            jax.ShapeDtypeStruct(expert_out.shape, BF16),
        ),
        in_specs=[pl.BlockSpec(memory_space=VMEM)] * 2 + [pl.BlockSpec(memory_space=pl.ANY)] * 2,
        out_specs=(
            pl.BlockSpec(memory_space=VMEM),
            pl.BlockSpec(memory_space=pl.ANY),
            pl.BlockSpec(memory_space=pl.ANY),
        ),
        scratch_shapes=[
            VMEM((2, 128, width), BF16),
            VMEM((2, 128, width), BF16),
            VMEM((2, 2, 2, 32, width), BF16),
            VMEM((2, 2, 4, 2, 32, width), BF16),
            VMEM(expert_in.shape, BF16),
            VMEM(expert_out.shape, BF16),
            VMEM((2, 256, hidden), BF16),
            VMEM((2, 256, hidden), F32),
            VMEM((2, 256, hidden), BF16),
            VMEM((2, 2, 4, 2, 32, width), BF16),
            VMEM((2, 2, 4, 32, width), BF16),
            VMEM((2, 4, 2, 32, width), BF16),
            VMEM((2, 2, 2, 32, width), BF16),
            VMEM((2, 2, 32, width), BF16),
            VMEM((2, 2, 2, 32, width), BF16),
            VMEM((2, 128, width), BF16),
            VMEM((2, 128, width), BF16),
            VMEM(expert_in.shape, BF16),
            VMEM(expert_out.shape, BF16),
            dma((2, 16)),
            dma((2, 16)),
            dma((2, 8)),
            dma((2, 8)),
            dma((2, 2)),
            dma((2, 2)),
            dma((2, 3)),
            dma((2, 3)),
            dma((2, 16)),
            dma((2, 16)),
            dma((2,)),
            dma((2, 2)),
        ],
        compiler_params=params(2, 50 << 20),
        name="experts",
    )(first, second, expert_in, expert_out)


def sum_kernel(
    g, u, out, u_out,
    ga, gq, gb, gh, gc, gt, gf, gv, gall,
    ua, uw, uc, ut, uz, uv, uall, uother,
    sg, rg, su, ru, s1, r1, s2, r2, s3, r3, s4, r4,
):
    z, core, xy = place()
    zl = lax.rem(z, 2)
    partner = at_core(flip(core))
    ring = [at_z(lax.rem(z + d, 4)) for d in range(1, 4)]
    greet([*ring, partner], xy)
    half = g.shape[2] // 2
    width = g.shape[3]
    chunk = 2 * half // 16
    wide = width // 4

    u_core = remote(u.at[flip(core)], ua, su.at[0], ru.at[0], partner)
    g_core = remote(g.at[:, flip(core)], ga, sg.at[0], rg.at[0], partner)
    u_core.start()
    g_core.start()

    u_swap = (xy, lambda k: uw.at[k], lambda k: uc.at[k], s1, r1)
    u_keep = pltpu.make_async_copy(uw.at[xy], uc.at[xy], s1.at[0])
    u_core.wait()
    for i in range(4):
        for j in range(4):
            where = (slice(8 * i, 8 * i + 8), slice(wide * j, wide * j + wide))
            uw[4 * i + j] = u[core, where[0], where[1]] + ua[where[0], where[1]]
    u_keep.start()
    xy_start(*u_swap)

    g_core.wait()
    gq[...] = (g[flip(zl), core].astype(F32) + ga[flip(zl)].astype(F32)).astype(BF16)
    g_mate = remote(
        gq.at[pl.ds(0, half)], gb.at[pl.ds(0, half)], sg.at[1], rg.at[1], at_z(mate(z))
    )
    g_cross = remote(
        gq.at[pl.ds(half, half)], gb.at[pl.ds(half, half)], sg.at[2], rg.at[2], at_z(cross(z))
    )
    g_mate.start()
    g_cross.start()

    u_keep.wait()
    xy_wait(*u_swap)
    ut[...] = jnp.sum(uc[...], axis=0)
    u_ring = [
        remote(ut, uz.at[z], su.at[d + 1], ru.at[d + 1], ring[d]) for d in range(3)
    ]
    u_mine = pltpu.make_async_copy(ut, uz.at[z], su.at[4])
    u_mine.start()
    for copy in u_ring:
        copy.start()

    g_mate.wait()
    g_cross.wait()
    gh[...] = (
        g[zl, core].astype(F32) + ga[zl].astype(F32) + gb[...].astype(F32)
    ).astype(BF16)
    g_swap = (
        xy,
        lambda k: gh.at[pl.ds(pl.multiple_of(chunk * k, chunk), chunk)],
        lambda k: gc.at[k],
        s2,
        r2,
    )
    g_keep = pltpu.make_async_copy(g_swap[1](xy), gc.at[xy], s2.at[0])
    g_keep.start()
    xy_start(*g_swap)

    u_mine.wait()
    for copy in u_ring:
        copy.wait()
    uv[...] = jnp.sum(uz[...], axis=0)
    u_back = (xy, lambda k: uv, lambda k: uall.at[k], s3, r3)
    u_stay = pltpu.make_async_copy(uv, uall.at[xy], s3.at[0])
    u_stay.start()
    xy_start(*u_back)

    g_keep.wait()
    xy_wait(*g_swap)
    total = gc[0].astype(F32)
    for k in range(1, 16):
        total = total + gc[k].astype(F32)
    gt[...] = total.astype(BF16)
    g_far = remote(gt, gf, sg.at[3], rg.at[3], at_z(far(z)))
    g_far.start()

    u_stay.wait()
    xy_wait(*u_back)
    u_other = remote(uall, uother, su.at[5], ru.at[5], partner)
    u_other.start()

    g_far.wait()
    gv[...] = (gt[...].astype(F32) + gf[...].astype(F32)).astype(BF16)
    g_back = (xy, lambda k: gv, lambda k: gall.at[k], s4, r4)
    g_stay = pltpu.make_async_copy(gv, gall.at[xy], s4.at[0])
    g_stay.start()
    xy_start(*g_back)

    u_other.wait()
    for i in range(4):
        for j in range(4):
            columns = slice(wide * j, wide * j + wide)
            rows = slice(8 * i, 8 * i + 8)
            u_out[core, rows, columns] = uall[4 * i + j]
            u_out[flip(core), rows, columns] = uother[4 * i + j]
    g_stay.wait()
    xy_wait(*g_back)
    for k in range(16):
        out[chunk * k : chunk * k + chunk] = gall[k].astype(F32)


def sums(partial, unit_partial):
    width = partial.shape[-1]
    rows = partial.shape[0] // 4
    chunk = rows // 16
    wide = width // 4
    dma = pltpu.SemaphoreType.DMA
    return pl.pallas_call(
        sum_kernel,
        out_shape=(
            jax.ShapeDtypeStruct((rows, width), F32),
            jax.ShapeDtypeStruct((2, 32, width), F32),
        ),
        in_specs=[pl.BlockSpec(memory_space=VMEM)] * 2,
        out_specs=(pl.BlockSpec(memory_space=VMEM), pl.BlockSpec(memory_space=VMEM)),
        scratch_shapes=[
            VMEM((2, rows, width), BF16),
            VMEM((rows, width), BF16),
            VMEM((rows, width), BF16),
            VMEM((rows, width), BF16),
            VMEM((16, chunk, width), BF16),
            VMEM((chunk, width), BF16),
            VMEM((chunk, width), BF16),
            VMEM((chunk, width), BF16),
            VMEM((16, chunk, width), BF16),
            VMEM((32, width), F32),
            VMEM((16, 8, wide), F32),
            VMEM((16, 8, wide), F32),
            VMEM((8, wide), F32),
            VMEM((4, 8, wide), F32),
            VMEM((8, wide), F32),
            VMEM((16, 8, wide), F32),
            VMEM((16, 8, wide), F32),
            dma((4,)),
            dma((4,)),
            dma((6,)),
            dma((6,)),
            *[dma((16,))] * 8,
        ],
        compiler_params=params(4),
        name="sums",
    )(partial.reshape(2, 2, rows, width), unit_partial.reshape(2, 32, width))


def shards(context, residual, cotangent, proj_weight, slot_params, expert_in, expert_out):
    images, tokens, width = context.shape
    rows = images * tokens
    slots = slot_params.shape[1]
    factor = logit_scale / math.sqrt(width)
    flat_ctx = context.reshape(rows, width)
    weight = whole_weight(proj_weight)
    mixed = jnp.dot(flat_ctx, weight, preferred_element_type=jnp.float32)
    stream = (residual.reshape(rows, width).astype(jnp.float32) + mixed).astype(jnp.bfloat16)
    stream32 = stream.astype(jnp.float32)
    inverse = lax.rsqrt(jnp.mean(stream32 * stream32, axis=-1, keepdims=True) + epsilon)
    normed32 = stream32 * inverse
    normed = normed32.astype(jnp.bfloat16)
    params32 = slot_params.astype(jnp.float32)
    slot_norm = jnp.sqrt(jnp.sum(params32 * params32, axis=0, keepdims=True) + epsilon)
    unit32 = params32 / slot_norm
    unit = unit32.astype(jnp.bfloat16)
    logits = factor * jnp.dot(normed, unit, preferred_element_type=jnp.float32)
    logits = logits.reshape(images, tokens, -1)
    expo = jnp.exp(logits)
    dispatch32 = expo / jnp.sum(expo, axis=1, keepdims=True)
    combine32 = expo / jnp.sum(expo, axis=2, keepdims=True)
    dispatch = dispatch32.astype(jnp.bfloat16)
    combine = combine32.astype(jnp.bfloat16)
    normed3 = normed.reshape(images, tokens, width)
    slot_in = jnp.einsum(
        "bms,bmd->bsd", dispatch, normed3, preferred_element_type=jnp.float32
    ).astype(jnp.bfloat16)
    grad_slot_out = jnp.einsum(
        "bms,bmd->bsd", combine, cotangent, preferred_element_type=jnp.float32
    ).astype(jnp.bfloat16)
    returned, grad_expert_in, grad_expert_out = experts(
        slot_in.reshape(images * slots, width),
        grad_slot_out.reshape(images * slots, width),
        expert_in,
        expert_out,
    )
    returned = returned.reshape(2, images, slots, width)
    slot_out, grad_slot_in = returned[0], returned[1]
    grad_combine = jnp.einsum(
        "bmd,bsd->bms", cotangent, slot_out, preferred_element_type=jnp.float32
    )
    grad_dispatch = jnp.einsum(
        "bmd,bsd->bms", normed3, grad_slot_in, preferred_element_type=jnp.float32
    )
    grad_logits32 = combine32 * (
        grad_combine - jnp.sum(combine32 * grad_combine, axis=2, keepdims=True)
    )
    grad_logits32 = grad_logits32 + dispatch32 * (
        grad_dispatch - jnp.sum(dispatch32 * grad_dispatch, axis=1, keepdims=True)
    )
    grad_logits = grad_logits32.astype(jnp.bfloat16).reshape(rows, -1)
    grad_normed = jnp.einsum(
        "bms,bsd->bmd", dispatch, grad_slot_in, preferred_element_type=jnp.float32
    ).reshape(rows, width)
    grad_normed = grad_normed + factor * jnp.dot(
        grad_logits, unit.T, preferred_element_type=jnp.float32
    )
    local_unit = jnp.dot(grad_logits.T, normed, preferred_element_type=jnp.float32)
    upstream = cotangent.reshape(rows, width).astype(jnp.float32)
    grad_stream = upstream + inverse * (
        grad_normed - normed32 * jnp.mean(normed32 * grad_normed, axis=-1, keepdims=True)
    )
    grad_residual = grad_stream.astype(jnp.bfloat16)
    grad_context = jnp.dot(
        grad_residual, weight.T, preferred_element_type=jnp.float32
    ).astype(jnp.bfloat16)
    partial = jnp.dot(
        flat_ctx.T, grad_residual, preferred_element_type=jnp.float32
    ).astype(jnp.bfloat16)
    grad_proj, unit_sum = sums(partial, local_unit)
    grad_unit = factor * unit_sum.reshape(slots, width).T
    grad_slots = (
        grad_unit - unit32 * jnp.sum(unit32 * grad_unit, axis=0, keepdims=True)
    ) / slot_norm
    return (
        grad_context.reshape(images, tokens, width),
        grad_residual.reshape(images, tokens, width),
        grad_proj,
        grad_slots,
        grad_expert_in,
        grad_expert_out,
    )


def solution(mesh):
    torus = Mesh(mesh.devices.reshape(2, 2, 4, 4, 2), AXES)
    placed = (
        P(IMG_EXP, None, None),
        P(IMG_EXP, None, None),
        P(IMG_EXP, None, None),
        P(IMG, None),
        P(),
        P(EXP, None, IMG),
        P(EXP, IMG, None),
    )
    return jax.shard_map(
        shards,
        mesh=torus,
        in_specs=placed,
        out_specs=(
            P(IMG_EXP, None, None),
            P(IMG_EXP, None, None),
            P(IMG, None),
            P(),
            P(EXP, None, IMG),
            P(EXP, IMG, None),
        ),
        check_vma=False,
    )
```

```python
import math

import jax
import jax.numpy as jnp
from jax import lax
from jax.experimental import pallas as pl
from jax.experimental.pallas import tpu as pltpu
from jax.sharding import Mesh
from jax.sharding import PartitionSpec as P

AXES = ("zl", "core", "x", "y", "zh")
IMG = ("zl", "core")
EXP = ("x", "y", "zh")
IMG_EXP = IMG + EXP
MESH = pl.DeviceIdType.MESH
VMEM = pltpu.VMEM
BF16 = jnp.bfloat16
F32 = jnp.float32


logit_scale = 48.0
epsilon = 1e-06


def place():
    zl, core, x, y, zh = (lax.axis_index(a) for a in AXES)
    return 2 * zh + zl, core, 4 * x + y


def flip(bit):
    return 1 - bit


def mate(z):
    return z + 1 - 2 * lax.rem(z, 2)


def cross(z):
    return 3 - z


def far(z):
    return lax.rem(z + 2, 4)


def at_z(z):
    return {"zl": lax.rem(z, 2), "zh": lax.div(z, 2)}


def at_core(core):
    return {"core": core}


def at_xy(k):
    return {"x": lax.div(k, 4), "y": lax.rem(k, 4)}


def remote(src, dst, send, recv, device):
    return pltpu.make_async_remote_copy(
        src_ref=src, dst_ref=dst, send_sem=send, recv_sem=recv, device_id=device, device_id_type=MESH
    )


def greet(devices, xy):
    barrier = pltpu.get_barrier_semaphore()
    for device in devices:
        pl.semaphore_signal(barrier, inc=1, device_id=device, device_id_type=MESH)

    def one(d, carry):
        pl.semaphore_signal(
            barrier, inc=1, device_id=at_xy(lax.rem(xy + d, 16)), device_id_type=MESH
        )
        return carry

    lax.fori_loop(1, 16, one, 0)
    return lambda: pl.semaphore_wait(barrier, len(devices) + 15)


def xy_copy(d, xy, src, dst, send, recv):
    k = lax.rem(xy + d, 16)
    return remote(src(k), dst(xy), send.at[d], recv.at[d], at_xy(k))


def xy_start(*args):
    def one(d, carry):
        xy_copy(d, *args).start()
        return carry

    lax.fori_loop(1, 16, one, 0)


def xy_wait(*args):
    def one(d, carry):
        xy_copy(d, *args).wait()
        return carry

    lax.fori_loop(1, 16, one, 0)


def rows8(ref, kind, k):
    return ref.at[kind, pl.ds(pl.multiple_of(8 * k, 8), 8)]


def one_hot(wanted):
    rows = lax.broadcasted_iota(jnp.int32, (128, 128), 0)
    columns = lax.broadcasted_iota(jnp.int32, (128, 128), 1)
    return (columns == wanted(rows)).astype(F32).astype(BF16)


def bits(value, low, count):
    return lax.rem(lax.div(value, 2**low), 2**count)


def to_pairs(r):
    return bits(r, 0, 1) * 64 + bits(r, 1, 6)


def from_pairs(r):
    return bits(r, 0, 6) * 2 + bits(r, 6, 1)


def to_blocks(r):
    return bits(r, 1, 4) * 8 + bits(r, 6, 1) * 4 + bits(r, 5, 1) * 2 + bits(r, 0, 1)


def from_blocks(r):
    return bits(r, 2, 1) * 64 + bits(r, 1, 1) * 32 + bits(r, 3, 4) * 2 + bits(r, 0, 1)


def reorder(wanted, rows):
    return jnp.dot(one_hot(wanted), rows, preferred_element_type=F32).astype(BF16)


def params(number, limit=None):
    return pltpu.CompilerParams(
        collective_id=number, has_side_effects=True, vmem_limit_bytes=limit or (40 << 20)
    )


def curve(x):
    slope = math.sqrt(2 / math.pi)
    square = x * x
    t = jnp.tanh(slope * (x + 0.044715 * (square * x)))
    cdf = 0.5 * (1.0 + t)
    return x * cdf, cdf + x * (0.5 * (1.0 - t * t)) * (slope * (1.0 + 3 * 0.044715 * square))


def times(a, b):
    return jnp.dot(a, b, preferred_element_type=F32)


def times_t(a, b):
    return lax.dot_general(a, b, (((1,), (1,)), ((), ())), preferred_element_type=F32)


def t_times(a, b):
    return lax.dot_general(a, b, (((0,), (0,)), ((), ())), preferred_element_type=F32)


def unit_of(slots_ref):
    params32 = slots_ref[...].astype(F32)
    norm = jnp.sqrt(jnp.sum(params32 * params32, axis=1, keepdims=True) + epsilon)
    return params32 / norm, norm


def inverse_of(stream32):
    return lax.rsqrt(jnp.mean(stream32 * stream32, axis=1, keepdims=True) + epsilon)


def expert_kernel(
    context, residual, cotangent, own, slots, win, wout,
    out, stream, normed, expo, whole, gin, gout,
    ctx, res, cot, natural,
    pairs, came, blocks, x, wi, wo, act, slope, gpre, o,
    halves, chip, paired, crossing, blocks2, pairs2, came2, gi, go,
    s1, r1, s2, r2, sa, ra, sb, rb, sc, rc, sw, sg, sp, rp,
):
    z, core, xy = place()
    zh = lax.div(z, 2)
    zl = lax.rem(z, 2)
    partner = at_core(flip(core))
    width = x.shape[-1]
    hidden = act.shape[-1]
    quarter = own.shape[0]
    half = quarter // 2
    entered = greet([at_z(mate(z)), at_z(cross(z)), partner], xy)

    def block_rows(block, start, size):
        return whole.at[pl.ds(pl.multiple_of(block * quarter + start, half), size)]

    block = 2 * zl + core
    load_ctx = pltpu.make_async_copy(context, ctx, sw.at[2])
    load_own = pltpu.make_async_copy(own, block_rows(block, 0, quarter), sw.at[3])
    load_res = pltpu.make_async_copy(residual, res, sw.at[4])
    load_cot = pltpu.make_async_copy(cotangent, cot, sw.at[5])
    load_in = pltpu.make_async_copy(win, wi, sw.at[0])
    load_out = pltpu.make_async_copy(wout, wo, sw.at[1])
    load_own.start()
    load_ctx.start()
    load_res.start()
    unit32, _ = unit_of(slots)
    unit = unit32.astype(BF16)
    entered()

    across = 2 * flip(zl) + core
    w_mate = remote(
        own.at[pl.ds(0, half)], block_rows(block, 0, half), sp.at[0], rp.at[0], at_z(mate(z))
    )
    w_cross = remote(
        own.at[pl.ds(half, half)], block_rows(block, half, half), sp.at[1], rp.at[1], at_z(cross(z))
    )
    w_core = remote(own, block_rows(block, 0, quarter), sp.at[2], rp.at[2], partner)
    w_first = remote(
        block_rows(across, 0, half), block_rows(across, 0, half), sp.at[3], rp.at[3], partner
    )
    w_second = remote(
        block_rows(across, half, half), block_rows(across, half, half), sp.at[4], rp.at[4], partner
    )
    w_mate.start()
    w_cross.start()
    w_core.start()
    load_cot.start()
    load_in.start()
    load_out.start()
    load_ctx.wait()
    load_res.wait()
    load_own.wait()

    def project(block, first=False):
        rows = whole[pl.ds(pl.multiple_of(block * quarter, quarter), quarter), :]
        for b in range(2):
            columns = ctx[b, :, pl.ds(pl.multiple_of(block * quarter, quarter), quarter)]
            start = res[b].astype(F32) if first else slope[b]
            slope[b] = start + times(columns, rows)

    project(block, True)
    w_core.wait_recv()
    project(2 * zl + flip(core))
    w_mate.wait_recv()
    w_first.start()
    w_cross.wait_recv()
    w_second.start()
    project(across)
    w_first.wait_recv()
    w_second.wait_recv()
    project(2 * flip(zl) + flip(core))

    def settle(i, carry):
        for b in range(2):
            rows = pl.ds(pl.multiple_of(i * 64, 64), 64)
            rounded = slope[b, rows, :].astype(BF16)
            stream[b, rows, :] = rounded
            stream32 = rounded.astype(F32)
            normed[b, rows, :] = (stream32 * inverse_of(stream32)).astype(BF16)
        return carry

    lax.fori_loop(0, 4, settle, 0)
    factor = logit_scale / math.sqrt(width)
    for b in range(2):
        rows = normed[b]
        ex = jnp.exp(factor * times_t(unit, rows))
        expo[b] = ex
        dispatch = (ex / jnp.sum(ex, axis=1, keepdims=True)).astype(BF16)
        natural[0, 64 * b : 64 * b + 64] = times(dispatch, rows).astype(BF16)
    pairs[0] = reorder(to_pairs, natural[0])

    def swap(kind):
        return (
            xy,
            lambda k: rows8(pairs, kind, k),
            lambda k: rows8(came, kind, k),
            s1.at[kind],
            r1.at[kind],
        )

    def keep(kind):
        return pltpu.make_async_copy(
            rows8(pairs, kind, xy), rows8(came, kind, xy), s1.at[kind, 0]
        )

    keep(0).start()
    xy_start(*swap(0))
    load_cot.wait()
    for b in range(2):
        ex = expo[b]
        combine = (ex / jnp.sum(ex, axis=0, keepdims=True)).astype(BF16)
        natural[1, 64 * b : 64 * b + 64] = times(combine, cot[b]).astype(BF16)
    pairs[1] = reorder(to_pairs, natural[1])
    keep(1).start()
    xy_start(*swap(1))

    def there(kind, zz):
        return x.at[kind, :, zz, core]

    def send(kind, number, src, zz, device):
        return remote(src, there(kind, zz), s2.at[kind, number], r2.at[kind, number], device)

    c, m, f = cross(z), mate(z), far(z)

    def to_mate(kind):
        return send(kind, 0, blocks.at[kind, zh], z, at_z(m))

    def to_cross(kind):
        return send(kind, 1, blocks.at[kind, flip(zh)], z, at_z(c))

    def on_mate(kind):
        return send(kind, 2, there(kind, c), c, at_z(m))

    def to_core(kind, number):
        if number == 3:
            return send(kind, 3, blocks.at[kind, zh], z, partner)
        zz = (c, m, f)[number - 4]
        return send(kind, number, there(kind, zz), zz, partner)

    def mine(kind):
        return pltpu.make_async_copy(blocks.at[kind, zh], there(kind, z), s2.at[kind, 7])

    def spread(kind):
        keep(kind).wait()
        xy_wait(*swap(kind))
        ordered = reorder(to_blocks, came[kind])
        for i in range(2):
            for e in range(2):
                blocks[kind, i, e] = ordered[i * 64 + e * 32 : i * 64 + e * 32 + 32]
        to_cross(kind).start()
        to_mate(kind).start()
        to_core(kind, 3).start()
        mine(kind).start()

    def relay(kind):
        to_cross(kind).wait_recv()
        on_mate(kind).start()
        to_core(kind, 4).start()
        to_mate(kind).wait_recv()
        to_core(kind, 5).start()

    def relay_last(kind):
        on_mate(kind).wait_recv()
        to_core(kind, 6).start()

    def arrived(kind):
        mine(kind).wait()
        for number in range(3, 7):
            to_core(kind, number).wait_recv()

    def sent(kind):
        to_mate(kind).wait_send()
        to_cross(kind).wait_send()
        on_mate(kind).wait_send()
        for number in range(3, 7):
            to_core(kind, number).wait_send()

    spread(0)
    spread(1)
    relay(0)
    relay(1)
    relay_last(0)
    arrived(0)
    load_in.wait()
    load_out.wait()

    def rows_of(kind, e):
        return x[kind, e].reshape(256, width)

    cut = 512

    def up(e):
        rows = rows_of(0, e)
        for n in range(0, hidden, cut):
            value, rise = curve(times(rows, wi[e, :, n : n + cut]))
            act[e, :, n : n + cut] = value.astype(BF16)
            slope[e, :, n : n + cut] = rise

    def down(e):
        rows = act[e]
        for n in range(0, width, cut):
            part = times(rows, wo[e, :, n : n + cut]).astype(BF16)
            o[0, e, :, :, :, n : n + cut] = part.reshape(4, 2, 32, cut)

    def back_down(e):
        rows = rows_of(1, e)
        for n in range(0, hidden, cut):
            rise = times_t(rows, wo[e, n : n + cut, :])
            gpre[e, :, n : n + cut] = (rise * slope[e, :, n : n + cut]).astype(BF16)

    def back_up(e):
        rows = gpre[e]
        for n in range(0, width, cut):
            part = times_t(rows, wi[e, n : n + cut, :]).astype(BF16)
            o[1, e, :, :, :, n : n + cut] = part.reshape(4, 2, 32, cut)

    def home_core(kind, e):
        return remote(
            o.at[kind, e, :, flip(core)], halves.at[kind, e], sa.at[kind, e], ra.at[kind, e], partner
        )

    def home_mate(kind):
        return [
            remote(chip.at[kind, zz], paired.at[kind, i], sb.at[kind, i], rb.at[kind, i], at_z(m))
            for i, zz in enumerate((f, m))
        ]

    def home_cross(kind):
        return remote(
            crossing.at[kind], blocks2.at[kind, zh], sb.at[kind, 2], rb.at[kind, 2], at_z(c)
        )

    def home_swap(kind):
        return (
            xy,
            lambda k: rows8(pairs2, kind, k),
            lambda k: rows8(came2, kind, k),
            sc.at[kind],
            rc.at[kind],
        )

    def home_keep(kind):
        return pltpu.make_async_copy(
            rows8(pairs2, kind, xy), rows8(came2, kind, xy), sc.at[kind, 0]
        )

    def chip_sum(kind):
        for e in range(2):
            home_core(kind, e).wait()
            for zz in range(4):
                chip[kind, zz, e] = (
                    o[kind, e, zz, core].astype(F32) + halves[kind, e, zz].astype(F32)
                ).astype(BF16)
        for copy in home_mate(kind):
            copy.start()

    def pair_sum(kind):
        on, own = home_mate(kind)
        on.wait_recv()
        for e in range(2):
            crossing[kind, e] = (
                chip[kind, c, e].astype(F32) + paired[kind, 0, e].astype(F32)
            ).astype(BF16)
        home_cross(kind).start()
        own.wait_recv()
        for e in range(2):
            blocks2[kind, zh, e] = (
                chip[kind, z, e].astype(F32) + paired[kind, 1, e].astype(F32)
            ).astype(BF16)

    def home(kind):
        home_cross(kind).wait_recv()
        rows = jnp.concatenate([blocks2[kind, i, e] for i in range(2) for e in range(2)], axis=0)
        pairs2[kind] = reorder(from_blocks, rows)
        home_keep(kind).start()
        xy_start(*home_swap(kind))

    def landed(kind):
        home_keep(kind).wait()
        xy_wait(*home_swap(kind))
        out[kind] = reorder(from_pairs, came2[kind])

    def out_gradient(e):
        right = rows_of(1, e)
        for n in range(0, hidden, cut):
            go[e, n : n + cut, :] = t_times(act[e, :, n : n + cut], right).astype(BF16)
        pltpu.make_async_copy(go.at[e], gout.at[e], sg.at[0, e]).start()

    def in_gradient(e):
        left = rows_of(0, e)
        right = gpre[e]
        for n in range(0, width, cut):
            gi[e, n : n + cut, :] = t_times(left[:, n : n + cut], right).astype(BF16)
        pltpu.make_async_copy(gi.at[e], gin.at[e], sg.at[1, e]).start()

    up(0)
    up(1)
    relay_last(1)
    for e in range(2):
        down(e)
        home_core(0, e).start()
    arrived(1)
    back_down(0)
    back_down(1)
    chip_sum(0)
    for e in range(2):
        back_up(e)
        home_core(1, e).start()
    out_gradient(0)
    chip_sum(1)
    pair_sum(0)
    out_gradient(1)
    pair_sum(1)
    home(0)
    in_gradient(0)
    home(1)
    in_gradient(1)
    landed(0)
    landed(1)
    for copy in (w_mate, w_cross, w_core, w_first, w_second):
        copy.wait_send()
    for kind in range(2):
        sent(kind)
        for copy in home_mate(kind):
            copy.wait_send()
        home_cross(kind).wait_send()
    for e in range(2):
        pltpu.make_async_copy(go.at[e], gout.at[e], sg.at[0, e]).wait()
        pltpu.make_async_copy(gi.at[e], gin.at[e], sg.at[1, e]).wait()


def experts(context, residual, cotangent, own, slots, expert_in, expert_out):
    width = context.shape[-1]
    hidden = expert_in.shape[-1]
    dma = pltpu.SemaphoreType.DMA
    whole = pl.BlockSpec(memory_space=VMEM)
    anywhere = pl.BlockSpec(memory_space=pl.ANY)
    return pl.pallas_call(
        expert_kernel,
        out_shape=(
            jax.ShapeDtypeStruct((2, 128, width), BF16),
            jax.ShapeDtypeStruct(context.shape, BF16),
            jax.ShapeDtypeStruct(context.shape, BF16),
            jax.ShapeDtypeStruct((2, 64, 256), F32),
            jax.ShapeDtypeStruct((width, width), BF16),
            jax.ShapeDtypeStruct(expert_in.shape, BF16),
            jax.ShapeDtypeStruct(expert_out.shape, BF16),
        ),
        in_specs=[anywhere] * 4 + [whole] + [anywhere] * 2,
        out_specs=(whole,) * 5 + (anywhere,) * 2,
        scratch_shapes=[
            VMEM(context.shape, BF16),
            VMEM(context.shape, BF16),
            VMEM(context.shape, BF16),
            VMEM((2, 128, width), BF16),
            VMEM((2, 128, width), BF16),
            VMEM((2, 128, width), BF16),
            VMEM((2, 2, 2, 32, width), BF16),
            VMEM((2, 2, 4, 2, 32, width), BF16),
            VMEM(expert_in.shape, BF16),
            VMEM(expert_out.shape, BF16),
            VMEM((2, 256, hidden), BF16),
            VMEM((2, 256, hidden), F32),
            VMEM((2, 256, hidden), BF16),
            VMEM((2, 2, 4, 2, 32, width), BF16),
            VMEM((2, 2, 4, 32, width), BF16),
            VMEM((2, 4, 2, 32, width), BF16),
            VMEM((2, 2, 2, 32, width), BF16),
            VMEM((2, 2, 32, width), BF16),
            VMEM((2, 2, 2, 32, width), BF16),
            VMEM((2, 128, width), BF16),
            VMEM((2, 128, width), BF16),
            VMEM(expert_in.shape, BF16),
            VMEM(expert_out.shape, BF16),
            dma((2, 16)),
            dma((2, 16)),
            dma((2, 8)),
            dma((2, 8)),
            dma((2, 2)),
            dma((2, 2)),
            dma((2, 3)),
            dma((2, 3)),
            dma((2, 16)),
            dma((2, 16)),
            dma((6,)),
            dma((2, 2)),
            dma((5,)),
            dma((5,)),
        ],
        compiler_params=params(2, 50 << 20),
        name="experts",
    )(context, residual, cotangent, own, slots, expert_in, expert_out)


def sum_kernel(
    back, stream, normed, expo, whole, slots, context, cotangent,
    gctx, gres, out, u_out,
    ctx, cot, gn, unit_part,
    gs, ga, mine, gq, gb, gh, gc, gt, gf, gv, gall,
    ua, uw, uc, ut, uz, uv, uall, uother,
    sw, sg, rg, su, ru, s1, r1, s2, r2, s3, r3, s4, r4,
):
    z, core, xy = place()
    zl = lax.rem(z, 2)
    partner = at_core(flip(core))
    ring = [at_z(lax.rem(z + d, 4)) for d in range(1, 4)]
    entered = greet([*ring, partner], xy)
    width = stream.shape[-1]
    quarter = width // 4
    half = quarter // 2
    chunk = quarter // 16
    wide = width // 4
    cut = width // 2
    factor = logit_scale / math.sqrt(width)
    load_ctx = pltpu.make_async_copy(context, ctx, sw.at[0])
    load_cot = pltpu.make_async_copy(cotangent, cot, sw.at[1])
    load_cot.start()
    load_ctx.start()
    unit32, norm = unit_of(slots)
    unit = unit32.astype(BF16)
    load_cot.wait()
    for b in range(2):
        ex = expo[b]
        dispatch32 = ex / jnp.sum(ex, axis=1, keepdims=True)
        combine32 = ex / jnp.sum(ex, axis=0, keepdims=True)
        grad_in = back[1, 64 * b : 64 * b + 64]
        grad_combine = times_t(back[0, 64 * b : 64 * b + 64], cot[b])
        grad_dispatch = times_t(grad_in, normed[b])
        grad_logits = combine32 * (
            grad_combine - jnp.sum(combine32 * grad_combine, axis=0, keepdims=True)
        )
        grad_logits = grad_logits + dispatch32 * (
            grad_dispatch - jnp.sum(dispatch32 * grad_dispatch, axis=1, keepdims=True)
        )
        grad_logits = grad_logits.astype(BF16)
        part = times(grad_logits, normed[b])
        for i in range(2):
            rows = part[32 * i : 32 * i + 32]
            unit_part[i] = rows if b == 0 else unit_part[i] + rows
        gn[b] = t_times(dispatch32.astype(BF16), grad_in) + factor * t_times(grad_logits, unit)
    entered()
    u_core = remote(unit_part.at[flip(core)], ua, su.at[0], ru.at[0], partner)
    u_core.start()

    def settle(i, carry):
        for b in range(2):
            rows = pl.ds(pl.multiple_of(i * 64, 64), 64)
            stream32 = stream[b, rows, :].astype(F32)
            inverse = inverse_of(stream32)
            normed32 = stream32 * inverse
            grad = gn[b, rows, :]
            pull = jnp.mean(normed32 * grad, axis=1, keepdims=True)
            gres[b, rows, :] = (
                cot[b, rows, :].astype(F32) + inverse * (grad - normed32 * pull)
            ).astype(BF16)
        return carry

    lax.fori_loop(0, 4, settle, 0)

    load_ctx.wait()

    def proj(block, h):
        left = ctx[:, :, pl.ds(pl.multiple_of(block * quarter, quarter), quarter)]
        right = gres[:, :, cut * h : cut * h + cut]
        return t_times(left.reshape(512, quarter), right.reshape(512, cut))

    def g_core(h, i):
        return remote(gs.at[h, i], ga.at[h, i], sg.at[h, i], rg.at[h, i], partner)

    def g_mate(h):
        return remote(
            gq.at[h, pl.ds(0, half)], gb.at[h, pl.ds(0, half)], sg.at[h, 2], rg.at[h, 2], at_z(mate(z))
        )

    def g_cross(h):
        return remote(
            gq.at[h, pl.ds(half, half)],
            gb.at[h, pl.ds(half, half)],
            sg.at[h, 3],
            rg.at[h, 3],
            at_z(cross(z)),
        )

    def g_swap(h):
        return (
            xy,
            lambda k: gh.at[h, pl.ds(pl.multiple_of(chunk * k, chunk), chunk)],
            lambda k: gc.at[h, k],
            s2.at[h],
            r2.at[h],
        )

    def g_keep(h):
        return pltpu.make_async_copy(g_swap(h)[1](xy), gc.at[h, xy], s2.at[h, 0])

    def g_far(h):
        return remote(gt.at[h], gf.at[h], sg.at[h, 4], rg.at[h, 4], at_z(far(z)))

    def g_back(h):
        return (xy, lambda k: gv.at[h], lambda k: gall.at[h, k], s4.at[h], r4.at[h])

    def g_stay(h):
        return pltpu.make_async_copy(gv.at[h], gall.at[h, xy], s4.at[h, 0])

    blocks = (2 * flip(zl), 2 * zl)
    u_swap = (xy, lambda k: uw.at[k], lambda k: uc.at[k], s1, r1)
    u_keep = pltpu.make_async_copy(uw.at[xy], uc.at[xy], s1.at[0])

    for h in range(2):
        gs[h, 0] = proj(blocks[0] + flip(core), h).astype(BF16)
        g_core(h, 0).start()
    u_core.wait()
    for i in range(4):
        for j in range(4):
            rows, columns = slice(8 * i, 8 * i + 8), slice(wide * j, wide * j + wide)
            uw[4 * i + j] = unit_part[core, rows, columns] + ua[rows, columns]
    u_keep.start()
    xy_start(*u_swap)
    for h in range(2):
        part = proj(blocks[0] + core, h)
        g_core(h, 0).wait()
        gq[h] = (part + ga[h, 0].astype(F32)).astype(BF16)
        g_mate(h).start()
        g_cross(h).start()
    for h in range(2):
        gs[h, 1] = proj(blocks[1] + flip(core), h).astype(BF16)
        g_core(h, 1).start()
    for h in range(2):
        mine[h] = proj(blocks[1] + core, h)
    u_keep.wait()
    xy_wait(*u_swap)
    ut[...] = jnp.sum(uc[...], axis=0)
    u_ring = [remote(ut, uz.at[z], su.at[d + 1], ru.at[d + 1], ring[d]) for d in range(3)]
    u_mine = pltpu.make_async_copy(ut, uz.at[z], su.at[4])
    u_mine.start()
    for copy in u_ring:
        copy.start()

    for h in range(2):
        g_core(h, 1).wait()
        g_mate(h).wait()
        g_cross(h).wait()
        gh[h] = (mine[h] + ga[h, 1].astype(F32) + gb[h].astype(F32)).astype(BF16)
        g_keep(h).start()
        xy_start(*g_swap(h))

    for b in range(2):
        for n in range(0, width, cut):
            gctx[b, :, n : n + cut] = times_t(gres[b], whole[n : n + cut, :]).astype(BF16)

    u_mine.wait()
    for copy in u_ring:
        copy.wait()
    uv[...] = jnp.sum(uz[...], axis=0)
    u_back = (xy, lambda k: uv, lambda k: uall.at[k], s3, r3)
    u_stay = pltpu.make_async_copy(uv, uall.at[xy], s3.at[0])
    u_stay.start()
    xy_start(*u_back)

    for h in range(2):
        g_keep(h).wait()
        xy_wait(*g_swap(h))
        total = gc[h, 0].astype(F32)
        for k in range(1, 16):
            total = total + gc[h, k].astype(F32)
        gt[h] = total.astype(BF16)
        g_far(h).start()

    u_stay.wait()
    xy_wait(*u_back)
    u_other = remote(uall, uother, su.at[5], ru.at[5], partner)
    u_other.start()

    for h in range(2):
        g_far(h).wait()
        gv[h] = (gt[h].astype(F32) + gf[h].astype(F32)).astype(BF16)
        g_stay(h).start()
        xy_start(*g_back(h))

    u_other.wait()
    for i in range(4):
        for j in range(4):
            columns = slice(wide * j, wide * j + wide)
            rows = slice(8 * i, 8 * i + 8)
            unit_part[core, rows, columns] = uall[4 * i + j]
            unit_part[flip(core), rows, columns] = uother[4 * i + j]
    grad_unit = factor * unit_part[...].reshape(64, width)
    u_out[...] = (
        grad_unit - unit32 * jnp.sum(unit32 * grad_unit, axis=1, keepdims=True)
    ) / norm
    for h in range(2):
        g_stay(h).wait()
        xy_wait(*g_back(h))
        for k in range(16):
            out[chunk * k : chunk * k + chunk, cut * h : cut * h + cut] = gall[h, k].astype(F32)


def sums(back, stream, normed, expo, whole, slots, context, cotangent):
    width = stream.shape[-1]
    rows = width // 4
    chunk = rows // 16
    wide = width // 4
    cut = width // 2
    dma = pltpu.SemaphoreType.DMA
    here = pl.BlockSpec(memory_space=VMEM)
    anywhere = pl.BlockSpec(memory_space=pl.ANY)
    return pl.pallas_call(
        sum_kernel,
        out_shape=(
            jax.ShapeDtypeStruct(context.shape, BF16),
            jax.ShapeDtypeStruct(context.shape, BF16),
            jax.ShapeDtypeStruct((rows, width), F32),
            jax.ShapeDtypeStruct((64, width), F32),
        ),
        in_specs=[here] * 6 + [anywhere] * 2,
        out_specs=(here,) * 4,
        scratch_shapes=[
            VMEM(context.shape, BF16),
            VMEM(context.shape, BF16),
            VMEM(context.shape, F32),
            VMEM((2, 32, width), F32),
            VMEM((2, 2, rows, cut), BF16),
            VMEM((2, 2, rows, cut), BF16),
            VMEM((2, rows, cut), F32),
            VMEM((2, rows, cut), BF16),
            VMEM((2, rows, cut), BF16),
            VMEM((2, rows, cut), BF16),
            VMEM((2, 16, chunk, cut), BF16),
            VMEM((2, chunk, cut), BF16),
            VMEM((2, chunk, cut), BF16),
            VMEM((2, chunk, cut), BF16),
            VMEM((2, 16, chunk, cut), BF16),
            VMEM((32, width), F32),
            VMEM((16, 8, wide), F32),
            VMEM((16, 8, wide), F32),
            VMEM((8, wide), F32),
            VMEM((4, 8, wide), F32),
            VMEM((8, wide), F32),
            VMEM((16, 8, wide), F32),
            VMEM((16, 8, wide), F32),
            dma((2,)),
            dma((2, 5)),
            dma((2, 5)),
            dma((6,)),
            dma((6,)),
            dma((16,)),
            dma((16,)),
            dma((2, 16)),
            dma((2, 16)),
            dma((16,)),
            dma((16,)),
            dma((2, 16)),
            dma((2, 16)),
        ],
        compiler_params=params(4, 36 << 20),
        name="sums",
    )(back, stream, normed, expo, whole, slots, context, cotangent)


def shards(context, residual, cotangent, proj_weight, slot_params, expert_in, expert_out):
    slots = slot_params.T
    back, stream, normed, expo, whole, grad_expert_in, grad_expert_out = experts(
        context, residual, cotangent, proj_weight, slots, expert_in, expert_out
    )
    grad_context, grad_residual, grad_proj, grad_slots = sums(
        back, stream, normed, expo, whole, slots, context, cotangent
    )
    return grad_context, grad_residual, grad_proj, grad_slots.T, grad_expert_in, grad_expert_out


def solution(mesh):
    torus = Mesh(mesh.devices.reshape(2, 2, 4, 4, 2), AXES)
    placed = (
        P(IMG_EXP, None, None),
        P(IMG_EXP, None, None),
        P(IMG_EXP, None, None),
        P(IMG, None),
        P(),
        P(EXP, None, IMG),
        P(EXP, IMG, None),
    )
    return jax.shard_map(
        shards,
        mesh=torus,
        in_specs=placed,
        out_specs=(
            P(IMG_EXP, None, None),
            P(IMG_EXP, None, None),
            P(IMG, None),
            P(),
            P(EXP, None, IMG),
            P(EXP, IMG, None),
        ),
        check_vma=False,
    )
```

```python
import math

import jax
import jax.numpy as jnp
from jax import lax
from jax.experimental import pallas as pl
from jax.experimental.pallas import tpu as pltpu
from jax.sharding import Mesh
from jax.sharding import PartitionSpec as P

AXES = ("zl", "core", "x", "y", "zh")
IMG = ("zl", "core")
EXP = ("x", "y", "zh")
IMG_EXP = IMG + EXP
MESH = pl.DeviceIdType.MESH
VMEM = pltpu.VMEM
BF16 = jnp.bfloat16
F32 = jnp.float32


logit_scale = 48.0
epsilon = 1e-06


def place():
    zl, core, x, y, zh = (lax.axis_index(a) for a in AXES)
    return 2 * zh + zl, core, 4 * x + y


def flip(bit):
    return 1 - bit


def mate(z):
    return z + 1 - 2 * lax.rem(z, 2)


def cross(z):
    return 3 - z


def far(z):
    return lax.rem(z + 2, 4)


def at_z(z):
    return {"zl": lax.rem(z, 2), "zh": lax.div(z, 2)}


def at_core(core):
    return {"core": core}


def at_xy(k):
    return {"x": lax.div(k, 4), "y": lax.rem(k, 4)}


def remote(src, dst, send, recv, device):
    return pltpu.make_async_remote_copy(
        src_ref=src, dst_ref=dst, send_sem=send, recv_sem=recv, device_id=device, device_id_type=MESH
    )


def greet(devices, xy):
    barrier = pltpu.get_barrier_semaphore()
    for device in devices:
        pl.semaphore_signal(barrier, inc=1, device_id=device, device_id_type=MESH)

    def one(d, carry):
        pl.semaphore_signal(
            barrier, inc=1, device_id=at_xy(lax.rem(xy + d, 16)), device_id_type=MESH
        )
        return carry

    lax.fori_loop(1, 16, one, 0)
    return lambda: pl.semaphore_wait(barrier, len(devices) + 15)


def xy_copy(d, xy, src, dst, send, recv):
    k = lax.rem(xy + d, 16)
    return remote(src(k), dst(xy), send.at[d], recv.at[d], at_xy(k))


def xy_start(*args):
    def one(d, carry):
        xy_copy(d, *args).start()
        return carry

    lax.fori_loop(1, 16, one, 0)


def xy_wait(*args):
    def one(d, carry):
        xy_copy(d, *args).wait()
        return carry

    lax.fori_loop(1, 16, one, 0)


def rows8(ref, kind, k):
    return ref.at[kind, pl.ds(pl.multiple_of(8 * k, 8), 8)]


def one_hot(wanted):
    rows = lax.broadcasted_iota(jnp.int32, (128, 128), 0)
    columns = lax.broadcasted_iota(jnp.int32, (128, 128), 1)
    return (columns == wanted(rows)).astype(F32).astype(BF16)


def bits(value, low, count):
    return lax.rem(lax.div(value, 2**low), 2**count)


def to_pairs(r):
    return bits(r, 0, 1) * 64 + bits(r, 1, 6)


def from_pairs(r):
    return bits(r, 0, 6) * 2 + bits(r, 6, 1)


def to_blocks(r):
    return bits(r, 1, 4) * 8 + bits(r, 6, 1) * 4 + bits(r, 5, 1) * 2 + bits(r, 0, 1)


def from_blocks(r):
    return bits(r, 2, 1) * 64 + bits(r, 1, 1) * 32 + bits(r, 3, 4) * 2 + bits(r, 0, 1)


def reorder(wanted, rows):
    return jnp.dot(one_hot(wanted), rows, preferred_element_type=F32).astype(BF16)


def params(number, limit=None):
    return pltpu.CompilerParams(
        collective_id=number, has_side_effects=True, vmem_limit_bytes=limit or (40 << 20)
    )


def curve(x):
    slope = math.sqrt(2 / math.pi)
    square = x * x
    t = jnp.tanh(slope * (x + 0.044715 * (square * x)))
    cdf = 0.5 * (1.0 + t)
    return x * cdf, cdf + x * (0.5 * (1.0 - t * t)) * (slope * (1.0 + 3 * 0.044715 * square))


def times(a, b):
    return jnp.dot(a, b, preferred_element_type=F32)


def times_t(a, b):
    return lax.dot_general(a, b, (((1,), (1,)), ((), ())), preferred_element_type=F32)


def t_times(a, b):
    return lax.dot_general(a, b, (((0,), (0,)), ((), ())), preferred_element_type=F32)


PIECES = 4


def unit_of(slots_ref):
    params32 = slots_ref[...].astype(F32)
    norm = jnp.sqrt(jnp.sum(params32 * params32, axis=1, keepdims=True) + epsilon)
    return params32 / norm, norm


def inverse_of(stream32):
    return lax.rsqrt(jnp.mean(stream32 * stream32, axis=1, keepdims=True) + epsilon)


def expert_kernel(
    context, residual, cotangent, own, slots, win, wout,
    out, stream, normed, expo, whole, x, act, gpre,
    ctx, res, cot, slots_here, natural,
    pairs, came, blocks, wi, wo, slope, o,
    halves, chip, paired, crossing, blocks2, pairs2, came2,
    s1, r1, s2, r2, sa, ra, sb, rb, sc, rc, sw, sp, rp,
):
    z, core, xy = place()
    zh = lax.div(z, 2)
    zl = lax.rem(z, 2)
    partner = at_core(flip(core))
    width = x.shape[-1]
    hidden = act.shape[-1]
    quarter = own.shape[0]
    half = quarter // 2
    entered = greet([at_z(mate(z)), at_z(cross(z)), partner], xy)

    def block_rows(block, start, size):
        return whole.at[pl.ds(pl.multiple_of(block * quarter + start, half), size)]

    block = 2 * zl + core
    load_ctx = pltpu.make_async_copy(context, ctx, sw.at[2])
    load_own = pltpu.make_async_copy(own, block_rows(block, 0, quarter), sw.at[3])
    load_res = pltpu.make_async_copy(residual, res, sw.at[4])
    load_cot = pltpu.make_async_copy(cotangent, cot, sw.at[5])
    load_in = pltpu.make_async_copy(win, wi, sw.at[0])
    load_out = pltpu.make_async_copy(wout, wo, sw.at[1])
    load_slots = pltpu.make_async_copy(slots, slots_here, sw.at[6])
    load_slots.start()
    load_own.start()
    load_ctx.start()
    load_res.start()
    load_slots.wait()
    unit32, _ = unit_of(slots_here)
    unit = unit32.astype(BF16)
    entered()

    across = 2 * flip(zl) + core
    w_mate = remote(
        own.at[pl.ds(0, half)], block_rows(block, 0, half), sp.at[0], rp.at[0], at_z(mate(z))
    )
    w_cross = remote(
        own.at[pl.ds(half, half)], block_rows(block, half, half), sp.at[1], rp.at[1], at_z(cross(z))
    )
    w_core = remote(own, block_rows(block, 0, quarter), sp.at[2], rp.at[2], partner)
    w_first = remote(
        block_rows(across, 0, half), block_rows(across, 0, half), sp.at[3], rp.at[3], partner
    )
    w_second = remote(
        block_rows(across, half, half), block_rows(across, half, half), sp.at[4], rp.at[4], partner
    )
    w_mate.start()
    w_cross.start()
    w_core.start()
    load_cot.start()
    load_in.start()
    load_out.start()
    load_ctx.wait()
    load_res.wait()
    load_own.wait()

    def project(block, first=False):
        rows = whole[pl.ds(pl.multiple_of(block * quarter, quarter), quarter), :]
        for b in range(2):
            columns = ctx[b, :, pl.ds(pl.multiple_of(block * quarter, quarter), quarter)]
            start = res[b].astype(F32) if first else slope[b]
            slope[b] = start + times(columns, rows)

    project(block, True)
    w_core.wait_recv()
    project(2 * zl + flip(core))
    w_mate.wait_recv()
    w_first.start()
    w_cross.wait_recv()
    w_second.start()
    project(across)
    w_first.wait_recv()
    w_second.wait_recv()
    project(2 * flip(zl) + flip(core))

    def settle(i, carry):
        for b in range(2):
            rows = pl.ds(pl.multiple_of(i * 64, 64), 64)
            rounded = slope[b, rows, :].astype(BF16)
            stream[b, rows, :] = rounded
            stream32 = rounded.astype(F32)
            normed[b, rows, :] = (stream32 * inverse_of(stream32)).astype(BF16)
        return carry

    lax.fori_loop(0, 4, settle, 0)
    factor = logit_scale / math.sqrt(width)
    for b in range(2):
        rows = normed[b]
        ex = jnp.exp(factor * times_t(unit, rows))
        expo[b] = ex
        dispatch = (ex / jnp.sum(ex, axis=1, keepdims=True)).astype(BF16)
        natural[0, 64 * b : 64 * b + 64] = times(dispatch, rows).astype(BF16)
    pairs[0] = reorder(to_pairs, natural[0])

    def swap(kind):
        return (
            xy,
            lambda k: rows8(pairs, kind, k),
            lambda k: rows8(came, kind, k),
            s1.at[kind],
            r1.at[kind],
        )

    def keep(kind):
        return pltpu.make_async_copy(
            rows8(pairs, kind, xy), rows8(came, kind, xy), s1.at[kind, 0]
        )

    keep(0).start()
    xy_start(*swap(0))
    load_cot.wait()
    for b in range(2):
        ex = expo[b]
        combine = (ex / jnp.sum(ex, axis=0, keepdims=True)).astype(BF16)
        natural[1, 64 * b : 64 * b + 64] = times(combine, cot[b]).astype(BF16)
    pairs[1] = reorder(to_pairs, natural[1])
    keep(1).start()
    xy_start(*swap(1))

    def there(kind, zz):
        return x.at[kind, :, zz, core]

    def send(kind, number, src, zz, device):
        return remote(src, there(kind, zz), s2.at[kind, number], r2.at[kind, number], device)

    c, m, f = cross(z), mate(z), far(z)

    def to_mate(kind):
        return send(kind, 0, blocks.at[kind, zh], z, at_z(m))

    def to_cross(kind):
        return send(kind, 1, blocks.at[kind, flip(zh)], z, at_z(c))

    def on_mate(kind):
        return send(kind, 2, there(kind, c), c, at_z(m))

    def to_core(kind, number):
        if number == 3:
            return send(kind, 3, blocks.at[kind, zh], z, partner)
        zz = (c, m, f)[number - 4]
        return send(kind, number, there(kind, zz), zz, partner)

    def mine(kind):
        return pltpu.make_async_copy(blocks.at[kind, zh], there(kind, z), s2.at[kind, 7])

    def spread(kind):
        keep(kind).wait()
        xy_wait(*swap(kind))
        ordered = reorder(to_blocks, came[kind])
        for i in range(2):
            for e in range(2):
                blocks[kind, i, e] = ordered[i * 64 + e * 32 : i * 64 + e * 32 + 32]
        to_cross(kind).start()
        to_mate(kind).start()
        to_core(kind, 3).start()
        mine(kind).start()

    def relay(kind):
        to_cross(kind).wait_recv()
        on_mate(kind).start()
        to_core(kind, 4).start()
        to_mate(kind).wait_recv()
        to_core(kind, 5).start()

    def relay_last(kind):
        on_mate(kind).wait_recv()
        to_core(kind, 6).start()

    def arrived(kind):
        mine(kind).wait()
        for number in range(3, 7):
            to_core(kind, number).wait_recv()

    def sent(kind):
        to_mate(kind).wait_send()
        to_cross(kind).wait_send()
        on_mate(kind).wait_send()
        for number in range(3, 7):
            to_core(kind, number).wait_send()

    spread(0)
    spread(1)
    relay(0)
    relay(1)
    relay_last(0)
    arrived(0)
    load_in.wait()
    load_out.wait()

    def rows_of(kind, e):
        return x[kind, e].reshape(256, width)

    cut = 512

    def up(e):
        rows = rows_of(0, e)
        for n in range(0, hidden, cut):
            value, rise = curve(times(rows, wi[e, :, n : n + cut]))
            act[e, :, n : n + cut] = value.astype(BF16)
            slope[e, :, n : n + cut] = rise

    def down(e):
        rows = act[e]
        for n in range(0, width, cut):
            part = times(rows, wo[e, :, n : n + cut]).astype(BF16)
            o[0, e, :, :, :, n : n + cut] = part.reshape(4, 2, 32, cut)

    def back_down(e):
        rows = rows_of(1, e)
        for n in range(0, hidden, cut):
            rise = times_t(rows, wo[e, n : n + cut, :])
            gpre[e, :, n : n + cut] = (rise * slope[e, :, n : n + cut]).astype(BF16)

    def back_up(e):
        rows = gpre[e]
        for n in range(0, width, cut):
            part = times_t(rows, wi[e, n : n + cut, :]).astype(BF16)
            o[1, e, :, :, :, n : n + cut] = part.reshape(4, 2, 32, cut)

    def home_core(kind, e):
        return remote(
            o.at[kind, e, :, flip(core)], halves.at[kind, e], sa.at[kind, e], ra.at[kind, e], partner
        )

    def home_mate(kind):
        return [
            remote(chip.at[kind, zz], paired.at[kind, i], sb.at[kind, i], rb.at[kind, i], at_z(m))
            for i, zz in enumerate((f, m))
        ]

    def home_cross(kind):
        return remote(
            crossing.at[kind], blocks2.at[kind, zh], sb.at[kind, 2], rb.at[kind, 2], at_z(c)
        )

    def home_swap(kind):
        return (
            xy,
            lambda k: rows8(pairs2, kind, k),
            lambda k: rows8(came2, kind, k),
            sc.at[kind],
            rc.at[kind],
        )

    def home_keep(kind):
        return pltpu.make_async_copy(
            rows8(pairs2, kind, xy), rows8(came2, kind, xy), sc.at[kind, 0]
        )

    def chip_sum(kind):
        for e in range(2):
            home_core(kind, e).wait()
            for zz in range(4):
                chip[kind, zz, e] = (
                    o[kind, e, zz, core].astype(F32) + halves[kind, e, zz].astype(F32)
                ).astype(BF16)
        for copy in home_mate(kind):
            copy.start()

    def pair_sum(kind):
        on, own = home_mate(kind)
        on.wait_recv()
        for e in range(2):
            crossing[kind, e] = (
                chip[kind, c, e].astype(F32) + paired[kind, 0, e].astype(F32)
            ).astype(BF16)
        home_cross(kind).start()
        own.wait_recv()
        for e in range(2):
            blocks2[kind, zh, e] = (
                chip[kind, z, e].astype(F32) + paired[kind, 1, e].astype(F32)
            ).astype(BF16)

    def home(kind):
        home_cross(kind).wait_recv()
        rows = jnp.concatenate([blocks2[kind, i, e] for i in range(2) for e in range(2)], axis=0)
        pairs2[kind] = reorder(from_blocks, rows)
        home_keep(kind).start()
        xy_start(*home_swap(kind))

    def landed(kind):
        home_keep(kind).wait()
        xy_wait(*home_swap(kind))
        out[kind] = reorder(from_pairs, came2[kind])

    up(0)
    up(1)
    relay_last(1)
    for e in range(2):
        down(e)
        home_core(0, e).start()
    arrived(1)
    back_down(0)
    back_down(1)
    chip_sum(0)
    for e in range(2):
        back_up(e)
        home_core(1, e).start()
    chip_sum(1)
    pair_sum(0)
    pair_sum(1)
    home(0)
    home(1)
    landed(0)
    landed(1)
    for copy in (w_mate, w_cross, w_core, w_first, w_second):
        copy.wait_send()
    for kind in range(2):
        sent(kind)
        for copy in home_mate(kind):
            copy.wait_send()
        home_cross(kind).wait_send()


def experts(context, residual, cotangent, own, slots, expert_in, expert_out):
    width = context.shape[-1]
    hidden = expert_in.shape[-1]
    dma = pltpu.SemaphoreType.DMA
    here = pl.BlockSpec(memory_space=VMEM)
    afar = pl.BlockSpec(memory_space=pltpu.HBM)
    return pl.pallas_call(
        expert_kernel,
        out_shape=(
            jax.ShapeDtypeStruct((2, 128, width), BF16),
            jax.ShapeDtypeStruct(context.shape, BF16),
            jax.ShapeDtypeStruct(context.shape, BF16),
            jax.ShapeDtypeStruct((2, 64, 256), F32),
            jax.ShapeDtypeStruct((width, width), BF16),
            jax.ShapeDtypeStruct((2, 2, 4, 2, 32, width), BF16),
            jax.ShapeDtypeStruct((2, 256, hidden), BF16),
            jax.ShapeDtypeStruct((2, 256, hidden), BF16),
        ),
        in_specs=[afar] * 7,
        out_specs=(here,) * 8,
        scratch_shapes=[
            VMEM(context.shape, BF16),
            VMEM(context.shape, BF16),
            VMEM(context.shape, BF16),
            VMEM(slots.shape, BF16),
            VMEM((2, 128, width), BF16),
            VMEM((2, 128, width), BF16),
            VMEM((2, 128, width), BF16),
            VMEM((2, 2, 2, 32, width), BF16),
            VMEM(expert_in.shape, BF16),
            VMEM(expert_out.shape, BF16),
            VMEM((2, 256, hidden), F32),
            VMEM((2, 2, 4, 2, 32, width), BF16),
            VMEM((2, 2, 4, 32, width), BF16),
            VMEM((2, 4, 2, 32, width), BF16),
            VMEM((2, 2, 2, 32, width), BF16),
            VMEM((2, 2, 32, width), BF16),
            VMEM((2, 2, 2, 32, width), BF16),
            VMEM((2, 128, width), BF16),
            VMEM((2, 128, width), BF16),
            dma((2, 16)),
            dma((2, 16)),
            dma((2, 8)),
            dma((2, 8)),
            dma((2, 2)),
            dma((2, 2)),
            dma((2, 3)),
            dma((2, 3)),
            dma((2, 16)),
            dma((2, 16)),
            dma((7,)),
            dma((5,)),
            dma((5,)),
        ],
        compiler_params=params(2, 36 << 20),
        name="experts",
    )(context, residual, cotangent, own, slots, expert_in, expert_out)


def sum_kernel(
    back, stream, normed, expo, whole, slots, context, cotangent,
    gctx, gres, out, u_out,
    ctx, cot, slots_here, gn, unit_part,
    gs, ga, mine, gq, gb, gh, gc, gt, gf, gv, gall,
    ua, uw, uc, ut, uz, uv, uall, uother,
    sw, sg, rg, su, ru, s1, r1, s2, r2, s3, r3, s4, r4,
):
    z, core, xy = place()
    zl = lax.rem(z, 2)
    partner = at_core(flip(core))
    ring = [at_z(lax.rem(z + d, 4)) for d in range(1, 4)]
    entered = greet([*ring, partner], xy)
    width = stream.shape[-1]
    quarter = width // 4
    half = quarter // 2
    chunk = quarter // 16
    wide = width // 4
    cut = width // PIECES
    factor = logit_scale / math.sqrt(width)
    load_ctx = pltpu.make_async_copy(context, ctx, sw.at[0])
    load_cot = pltpu.make_async_copy(cotangent, cot, sw.at[1])
    load_slots = pltpu.make_async_copy(slots, slots_here, sw.at[2])
    load_slots.start()
    load_cot.start()
    load_ctx.start()
    load_slots.wait()
    unit32, norm = unit_of(slots_here)
    unit = unit32.astype(BF16)
    load_cot.wait()
    for b in range(2):
        ex = expo[b]
        dispatch32 = ex / jnp.sum(ex, axis=1, keepdims=True)
        combine32 = ex / jnp.sum(ex, axis=0, keepdims=True)
        grad_in = back[1, 64 * b : 64 * b + 64]
        grad_combine = times_t(back[0, 64 * b : 64 * b + 64], cot[b])
        grad_dispatch = times_t(grad_in, normed[b])
        grad_logits = combine32 * (
            grad_combine - jnp.sum(combine32 * grad_combine, axis=0, keepdims=True)
        )
        grad_logits = grad_logits + dispatch32 * (
            grad_dispatch - jnp.sum(dispatch32 * grad_dispatch, axis=1, keepdims=True)
        )
        grad_logits = grad_logits.astype(BF16)
        part = times(grad_logits, normed[b])
        for i in range(2):
            rows = part[32 * i : 32 * i + 32]
            unit_part[i] = rows if b == 0 else unit_part[i] + rows
        gn[b] = t_times(dispatch32.astype(BF16), grad_in) + factor * t_times(grad_logits, unit)
    entered()
    u_core = remote(unit_part.at[flip(core)], ua, su.at[0], ru.at[0], partner)
    u_core.start()

    def settle(i, carry):
        for b in range(2):
            rows = pl.ds(pl.multiple_of(i * 64, 64), 64)
            stream32 = stream[b, rows, :].astype(F32)
            inverse = inverse_of(stream32)
            normed32 = stream32 * inverse
            grad = gn[b, rows, :]
            pull = jnp.mean(normed32 * grad, axis=1, keepdims=True)
            gres[b, rows, :] = (
                cot[b, rows, :].astype(F32) + inverse * (grad - normed32 * pull)
            ).astype(BF16)
        return carry

    lax.fori_loop(0, 4, settle, 0)

    load_ctx.wait()

    def proj(block, h):
        left = ctx[:, :, pl.ds(pl.multiple_of(block * quarter, quarter), quarter)]
        right = gres[:, :, cut * h : cut * h + cut]
        return t_times(left.reshape(512, quarter), right.reshape(512, cut))

    def g_core(h, i):
        return remote(gs.at[h, i], ga.at[h, i], sg.at[h, i], rg.at[h, i], partner)

    def g_mate(h):
        return remote(
            gq.at[h, pl.ds(0, half)], gb.at[h, pl.ds(0, half)], sg.at[h, 2], rg.at[h, 2], at_z(mate(z))
        )

    def g_cross(h):
        return remote(
            gq.at[h, pl.ds(half, half)],
            gb.at[h, pl.ds(half, half)],
            sg.at[h, 3],
            rg.at[h, 3],
            at_z(cross(z)),
        )

    def g_swap(h):
        return (
            xy,
            lambda k: gh.at[h, pl.ds(pl.multiple_of(chunk * k, chunk), chunk)],
            lambda k: gc.at[h, k],
            s2.at[h],
            r2.at[h],
        )

    def g_keep(h):
        return pltpu.make_async_copy(g_swap(h)[1](xy), gc.at[h, xy], s2.at[h, 0])

    def g_far(h):
        return remote(gt.at[h], gf.at[h], sg.at[h, 4], rg.at[h, 4], at_z(far(z)))

    def g_back(h):
        return (xy, lambda k: gv.at[h], lambda k: gall.at[h, k], s4.at[h], r4.at[h])

    def g_stay(h):
        return pltpu.make_async_copy(gv.at[h], gall.at[h, xy], s4.at[h, 0])

    blocks = (2 * flip(zl), 2 * zl)
    u_swap = (xy, lambda k: uw.at[k], lambda k: uc.at[k], s1, r1)
    u_keep = pltpu.make_async_copy(uw.at[xy], uc.at[xy], s1.at[0])

    pieces = range(PIECES)
    for h in pieces:
        gs[h, 0] = proj(blocks[0] + flip(core), h).astype(BF16)
        g_core(h, 0).start()
    u_core.wait()
    for i in range(4):
        for j in range(4):
            rows, columns = slice(8 * i, 8 * i + 8), slice(wide * j, wide * j + wide)
            uw[4 * i + j] = unit_part[core, rows, columns] + ua[rows, columns]
    u_keep.start()
    xy_start(*u_swap)
    for h in pieces:
        part = proj(blocks[0] + core, h)
        g_core(h, 0).wait()
        gq[h] = (part + ga[h, 0].astype(F32)).astype(BF16)
        g_mate(h).start()
        g_cross(h).start()
    for h in pieces:
        gs[h, 1] = proj(blocks[1] + flip(core), h).astype(BF16)
        g_core(h, 1).start()
    for h in pieces:
        mine[h] = proj(blocks[1] + core, h)

    u_ring = [remote(ut, uz.at[z], su.at[d + 1], ru.at[d + 1], ring[d]) for d in range(3)]
    u_mine = pltpu.make_async_copy(ut, uz.at[z], su.at[4])
    u_back = (xy, lambda k: uv, lambda k: uall.at[k], s3, r3)
    u_stay = pltpu.make_async_copy(uv, uall.at[xy], s3.at[0])
    u_other = remote(uall, uother, su.at[5], ru.at[5], partner)

    def u_first():
        u_keep.wait()
        xy_wait(*u_swap)
        ut[...] = jnp.sum(uc[...], axis=0)
        u_mine.start()
        for copy in u_ring:
            copy.start()

    def u_second():
        u_mine.wait()
        for copy in u_ring:
            copy.wait()
        uv[...] = jnp.sum(uz[...], axis=0)
        u_stay.start()
        xy_start(*u_back)

    def u_third():
        u_stay.wait()
        xy_wait(*u_back)
        u_other.start()

    def chip_rows(h):
        g_core(h, 1).wait()
        g_mate(h).wait()
        g_cross(h).wait()
        gh[h] = (mine[h] + ga[h, 1].astype(F32) + gb[h].astype(F32)).astype(BF16)
        g_keep(h).start()
        xy_start(*g_swap(h))

    def plane_sum(h):
        g_keep(h).wait()
        xy_wait(*g_swap(h))
        total = gc[h, 0].astype(F32)
        for k in range(1, 16):
            total = total + gc[h, k].astype(F32)
        gt[h] = total.astype(BF16)
        g_far(h).start()

    def far_sum(h):
        g_far(h).wait()
        gv[h] = (gt[h].astype(F32) + gf[h].astype(F32)).astype(BF16)
        g_stay(h).start()
        xy_start(*g_back(h))

    def finish(h):
        g_stay(h).wait()
        xy_wait(*g_back(h))
        for k in range(16):
            out[chunk * k : chunk * k + chunk, cut * h : cut * h + cut] = gall[h, k].astype(F32)

    def grad_context(h):
        for b in range(2):
            columns = slice(cut * h, cut * h + cut)
            gctx[b, :, columns] = times_t(gres[b], whole[columns, :]).astype(BF16)

    for h in pieces:
        chip_rows(h)
        if h == 0:
            u_first()
        grad_context(h)
    u_second()
    for h in pieces:
        plane_sum(h)
        if h:
            far_sum(h - 1)
    far_sum(PIECES - 1)
    u_third()
    u_other.wait()
    for i in range(4):
        for j in range(4):
            columns = slice(wide * j, wide * j + wide)
            rows = slice(8 * i, 8 * i + 8)
            unit_part[core, rows, columns] = uall[4 * i + j]
            unit_part[flip(core), rows, columns] = uother[4 * i + j]
    grad_unit = factor * unit_part[...].reshape(64, width)
    u_out[...] = (
        grad_unit - unit32 * jnp.sum(unit32 * grad_unit, axis=1, keepdims=True)
    ) / norm
    for h in pieces:
        finish(h)


def sums(back, stream, normed, expo, whole, slots, context, cotangent):
    width = stream.shape[-1]
    rows = width // 4
    chunk = rows // 16
    wide = width // 4
    cut = width // PIECES
    dma = pltpu.SemaphoreType.DMA
    here = pl.BlockSpec(memory_space=VMEM)
    afar = pl.BlockSpec(memory_space=pltpu.HBM)
    return pl.pallas_call(
        sum_kernel,
        out_shape=(
            jax.ShapeDtypeStruct(context.shape, BF16),
            jax.ShapeDtypeStruct(context.shape, BF16),
            jax.ShapeDtypeStruct((rows, width), F32),
            jax.ShapeDtypeStruct((64, width), F32),
        ),
        in_specs=[here] * 5 + [afar] * 3,
        out_specs=(here,) * 4,
        scratch_shapes=[
            VMEM(context.shape, BF16),
            VMEM(context.shape, BF16),
            VMEM(slots.shape, BF16),
            VMEM(context.shape, F32),
            VMEM((2, 32, width), F32),
            VMEM((PIECES, 2, rows, cut), BF16),
            VMEM((PIECES, 2, rows, cut), BF16),
            VMEM((PIECES, rows, cut), F32),
            VMEM((PIECES, rows, cut), BF16),
            VMEM((PIECES, rows, cut), BF16),
            VMEM((PIECES, rows, cut), BF16),
            VMEM((PIECES, 16, chunk, cut), BF16),
            VMEM((PIECES, chunk, cut), BF16),
            VMEM((PIECES, chunk, cut), BF16),
            VMEM((PIECES, chunk, cut), BF16),
            VMEM((PIECES, 16, chunk, cut), BF16),
            VMEM((32, width), F32),
            VMEM((16, 8, wide), F32),
            VMEM((16, 8, wide), F32),
            VMEM((8, wide), F32),
            VMEM((4, 8, wide), F32),
            VMEM((8, wide), F32),
            VMEM((16, 8, wide), F32),
            VMEM((16, 8, wide), F32),
            dma((3,)),
            dma((PIECES, 5)),
            dma((PIECES, 5)),
            dma((6,)),
            dma((6,)),
            dma((16,)),
            dma((16,)),
            dma((PIECES, 16)),
            dma((PIECES, 16)),
            dma((16,)),
            dma((16,)),
            dma((PIECES, 16)),
            dma((PIECES, 16)),
        ],
        compiler_params=params(4, 28 << 20),
        name="sums",
    )(back, stream, normed, expo, whole, slots, context, cotangent)


def result_kernel(
    x, act, gpre, gctx, gres, gproj, gslots,
    to_ctx, to_res, to_proj, to_slots, to_in, to_out,
    gi, go, sem, wsem,
):
    width = x.shape[-1]
    cut = width // 2
    ready = [
        pltpu.make_async_copy(src, dst, sem.at[i])
        for i, (src, dst) in enumerate(
            ((gctx, to_ctx), (gres, to_res), (gproj, to_proj), (gslots, to_slots))
        )
    ]
    for copy in ready:
        copy.start()
    copies = []
    for e in range(2):
        first, second = (x[kind, e].reshape(256, width) for kind in range(2))
        for i in range(2):
            rows = pl.ds(cut * i, cut)
            go[e, rows, :] = t_times(act[e, :, rows], second).astype(BF16)
            copies.append(
                pltpu.make_async_copy(go.at[e, rows], to_out.at[e, rows], wsem.at[0, e, i])
            )
            copies[-1].start()
            gi[e, rows, :] = t_times(first[:, cut * i : cut * i + cut], gpre[e]).astype(BF16)
            copies.append(
                pltpu.make_async_copy(gi.at[e, rows], to_in.at[e, rows], wsem.at[1, e, i])
            )
            copies[-1].start()
    for copy in ready + copies:
        copy.wait()


def results(x, act, gpre, gctx, gres, gproj, gslots):
    width = x.shape[-1]
    hidden = act.shape[-1]
    dma = pltpu.SemaphoreType.DMA
    afar = pl.BlockSpec(memory_space=pltpu.HBM)
    shapes = (
        jax.ShapeDtypeStruct((2, width, hidden), BF16),
        jax.ShapeDtypeStruct((2, hidden, width), BF16),
    )
    return pl.pallas_call(
        result_kernel,
        out_shape=tuple(
            jax.ShapeDtypeStruct(a.shape, a.dtype) for a in (gctx, gres, gproj, gslots)
        )
        + shapes,
        in_specs=[pl.BlockSpec(memory_space=VMEM)] * 7,
        out_specs=(afar,) * 6,
        scratch_shapes=[
            VMEM(shapes[0].shape, BF16),
            VMEM(shapes[1].shape, BF16),
            dma((4,)),
            dma((2, 2, 2)),
        ],
        compiler_params=pltpu.CompilerParams(vmem_limit_bytes=24 << 20),
        name="results",
    )(x, act, gpre, gctx, gres, gproj, gslots)


def shards(context, residual, cotangent, proj_weight, slot_params, expert_in, expert_out):
    slots = slot_params.T
    context, residual, cotangent, proj_weight, slots, expert_in, expert_out = (
        pltpu.with_memory_space_constraint(a, pltpu.HBM)
        for a in (context, residual, cotangent, proj_weight, slots, expert_in, expert_out)
    )
    back, stream, normed, expo, whole, x, act, gpre = experts(
        context, residual, cotangent, proj_weight, slots, expert_in, expert_out
    )
    four = sums(back, stream, normed, expo, whole, slots, context, cotangent)
    grad_context, grad_residual, grad_proj, grad_slots, grad_in, grad_out = results(
        x, act, gpre, *four
    )
    return grad_context, grad_residual, grad_proj, grad_slots.T, grad_in, grad_out


def solution(mesh):
    torus = Mesh(mesh.devices.reshape(2, 2, 4, 4, 2), AXES)
    placed = (
        P(IMG_EXP, None, None),
        P(IMG_EXP, None, None),
        P(IMG_EXP, None, None),
        P(IMG, None),
        P(),
        P(EXP, None, IMG),
        P(EXP, IMG, None),
    )
    return jax.shard_map(
        shards,
        mesh=torus,
        in_specs=placed,
        out_specs=(
            P(IMG_EXP, None, None),
            P(IMG_EXP, None, None),
            P(IMG, None),
            P(),
            P(EXP, None, IMG),
            P(EXP, IMG, None),
        ),
        check_vma=False,
    )
```

```python
import math

import jax
import jax.numpy as jnp
from jax import lax
from jax.experimental import pallas as pl
from jax.experimental.pallas import tpu as pltpu
from jax.sharding import Mesh
from jax.sharding import PartitionSpec as P

AXES = ("zl", "core", "x", "y", "zh")
IMG = ("zl", "core")
EXP = ("x", "y", "zh")
IMG_EXP = IMG + EXP
MESH = pl.DeviceIdType.MESH
VMEM = pltpu.VMEM
BF16 = jnp.bfloat16
F32 = jnp.float32


logit_scale = 48.0
epsilon = 1e-06


def place():
    zl, core, x, y, zh = (lax.axis_index(a) for a in AXES)
    return 2 * zh + zl, core, 4 * x + y


def flip(bit):
    return 1 - bit


def mate(z):
    return z + 1 - 2 * lax.rem(z, 2)


def cross(z):
    return 3 - z


def far(z):
    return lax.rem(z + 2, 4)


def at_z(z):
    return {"zl": lax.rem(z, 2), "zh": lax.div(z, 2)}


def at_core(core):
    return {"core": core}


def at_xy(k):
    return {"x": lax.div(k, 4), "y": lax.rem(k, 4)}


def remote(src, dst, send, recv, device):
    return pltpu.make_async_remote_copy(
        src_ref=src, dst_ref=dst, send_sem=send, recv_sem=recv, device_id=device, device_id_type=MESH
    )


def greet(devices, xy=None):
    barrier = pltpu.get_barrier_semaphore()
    for device in devices:
        pl.semaphore_signal(barrier, inc=1, device_id=device, device_id_type=MESH)

    def one(d, carry):
        pl.semaphore_signal(
            barrier, inc=1, device_id=at_xy(lax.rem(xy + d, 16)), device_id_type=MESH
        )
        return carry

    if xy is None:
        return lambda: pl.semaphore_wait(barrier, len(devices))
    lax.fori_loop(1, 16, one, 0)
    return lambda: pl.semaphore_wait(barrier, len(devices) + 15)


def xy_copy(d, xy, src, dst, send, recv):
    k = lax.rem(xy + d, 16)
    return remote(src(k), dst(xy), send.at[d], recv.at[d], at_xy(k))


def xy_start(*args):
    def one(d, carry):
        xy_copy(d, *args).start()
        return carry

    lax.fori_loop(1, 16, one, 0)


def xy_wait(*args):
    def one(d, carry):
        xy_copy(d, *args).wait()
        return carry

    lax.fori_loop(1, 16, one, 0)


def rows8(ref, kind, k):
    return ref.at[kind, pl.ds(pl.multiple_of(8 * k, 8), 8)]


def one_hot(wanted):
    rows = lax.broadcasted_iota(jnp.int32, (128, 128), 0)
    columns = lax.broadcasted_iota(jnp.int32, (128, 128), 1)
    return (columns == wanted(rows)).astype(F32).astype(BF16)


def bits(value, low, count):
    return lax.rem(lax.div(value, 2**low), 2**count)


def to_pairs(r):
    return bits(r, 0, 1) * 64 + bits(r, 1, 6)


def from_pairs(r):
    return bits(r, 0, 6) * 2 + bits(r, 6, 1)


def to_blocks(r):
    return bits(r, 1, 4) * 8 + bits(r, 6, 1) * 4 + bits(r, 5, 1) * 2 + bits(r, 0, 1)


def from_blocks(r):
    return bits(r, 2, 1) * 64 + bits(r, 1, 1) * 32 + bits(r, 3, 4) * 2 + bits(r, 0, 1)


def reorder(wanted, rows):
    return jnp.dot(one_hot(wanted), rows, preferred_element_type=F32).astype(BF16)


def params(number, limit=None):
    return pltpu.CompilerParams(
        collective_id=number, has_side_effects=True, vmem_limit_bytes=limit or (40 << 20)
    )


def curve(x):
    slope = math.sqrt(2 / math.pi)
    square = x * x
    t = jnp.tanh(slope * (x + 0.044715 * (square * x)))
    cdf = 0.5 * (1.0 + t)
    return x * cdf, cdf + x * (0.5 * (1.0 - t * t)) * (slope * (1.0 + 3 * 0.044715 * square))


def times(a, b):
    return jnp.dot(a, b, preferred_element_type=F32)


def times_t(a, b):
    return lax.dot_general(a, b, (((1,), (1,)), ((), ())), preferred_element_type=F32)


def t_times(a, b):
    return lax.dot_general(a, b, (((0,), (0,)), ((), ())), preferred_element_type=F32)


PIECES = 4


def unit_of(slots_ref):
    params32 = slots_ref[...].astype(F32)
    norm = jnp.sqrt(jnp.sum(params32 * params32, axis=1, keepdims=True) + epsilon)
    return params32 / norm, norm


def inverse_of(stream32):
    return lax.rsqrt(jnp.mean(stream32 * stream32, axis=1, keepdims=True) + epsilon)


PARTS = 2
FIRST = 28


def project_kernel(
    context, residual, cotangent, own,
    whole, total, ctx, cot,
    res, sw, sp, rp,
):
    z, core, _ = place()
    zl = lax.rem(z, 2)
    partner = at_core(flip(core))
    quarter = own.shape[0]
    half = quarter // 2
    piece = half // PARTS
    entered = greet([at_z(mate(z)), at_z(cross(z)), partner])

    def block_rows(block, start, size):
        return whole.at[pl.ds(pl.multiple_of(block * quarter + start, piece), size)]

    block = 2 * zl + core
    load_ctx = pltpu.make_async_copy(context, ctx, sw.at[0])
    load_own = pltpu.make_async_copy(own, block_rows(block, 0, quarter), sw.at[1])
    load_res = pltpu.make_async_copy(residual, res, sw.at[2])
    load_cot = pltpu.make_async_copy(cotangent, cot, sw.at[3])
    load_own.start()
    load_ctx.start()
    load_res.start()
    entered()

    across = 2 * flip(zl) + core
    over, on = [], []
    for p in range(PARTS):
        for side, device in enumerate((at_z(mate(z)), at_z(cross(z)))):
            number = 2 * p + side
            start = side * half + p * piece
            over.append(
                remote(
                    own.at[pl.ds(start, piece)],
                    block_rows(block, start, piece),
                    sp.at[number],
                    rp.at[number],
                    device,
                )
            )
            rows = block_rows(across, start, piece)
            on.append(
                remote(rows, rows, sp.at[2 * PARTS + number], rp.at[2 * PARTS + number], partner)
            )
    w_core = remote(own, block_rows(block, 0, quarter), sp.at[4 * PARTS], rp.at[4 * PARTS], partner)
    for copy in over:
        copy.start()
    w_core.start()
    load_cot.start()
    load_ctx.wait()
    load_res.wait()
    load_own.wait()
    add_block(ctx, whole, block, total, lambda b: res[b].astype(F32))
    w_core.wait_recv()
    add_block(ctx, whole, 2 * zl + flip(core), total, lambda b: total[b])
    for first, second in zip(over, on):
        first.wait_recv()
        second.start()
    for copy in on:
        copy.wait()
    for copy in over:
        copy.wait_send()
    w_core.wait_send()
    load_cot.wait()


def add_block(ctx, whole, block, total, start):
    quarter = whole.shape[0] // 4
    span = pl.ds(pl.multiple_of(block * quarter, quarter), quarter)
    rows = whole[span, :]
    for b in range(2):
        total[b] = start(b) + times(ctx[b, :, span], rows)


def project(context, residual, cotangent, own):
    width = own.shape[-1]
    dma = pltpu.SemaphoreType.DMA
    afar = pl.BlockSpec(memory_space=pltpu.HBM)
    return pl.pallas_call(
        project_kernel,
        out_shape=(
            jax.ShapeDtypeStruct((width, width), BF16),
            jax.ShapeDtypeStruct(context.shape, F32),
            jax.ShapeDtypeStruct(context.shape, BF16),
            jax.ShapeDtypeStruct(context.shape, BF16),
        ),
        in_specs=[afar] * 4,
        out_specs=(pl.BlockSpec(memory_space=VMEM),) * 4,
        scratch_shapes=[
            VMEM(context.shape, BF16),
            dma((4,)),
            dma((4 * PARTS + 1,)),
            dma((4 * PARTS + 1,)),
        ],
        compiler_params=params(1, 12 << 20),
        name="project",
    )(context, residual, cotangent, own)


def expert_kernel(
    ctx, cot, whole, total, slots, win, wout,
    out, stream, normed, spread32, pulled, x, act, gpre,
    slots_here, natural, expo,
    pairs, came, blocks, wi, wo, slope, o,
    halves, chip, paired, crossing, blocks2, pairs2, came2,
    s1, r1, s2, r2, sa, ra, sb, rb, sc, rc, sw,
):
    z, core, xy = place()
    zh = lax.div(z, 2)
    zl = lax.rem(z, 2)
    partner = at_core(flip(core))
    width = x.shape[-1]
    hidden = act.shape[-1]
    entered = greet([at_z(mate(z)), at_z(cross(z)), at_z(far(z)), partner], xy)
    load_slots = pltpu.make_async_copy(slots, slots_here, sw.at[2])
    load_in = pltpu.make_async_copy(win, wi, sw.at[0])
    load_out = pltpu.make_async_copy(wout, wo, sw.at[1])
    load_slots.start()
    load_in.start()
    load_out.start()
    add_block(ctx, whole, 2 * flip(zl) + core, slope, lambda b: total[b])
    add_block(ctx, whole, 2 * flip(zl) + flip(core), slope, lambda b: slope[b])
    load_slots.wait()
    unit32, _ = unit_of(slots_here)
    unit = unit32.astype(BF16)

    def settle(i, carry):
        for b in range(2):
            rows = pl.ds(pl.multiple_of(i * 64, 64), 64)
            rounded = slope[b, rows, :].astype(BF16)
            stream[b, rows, :] = rounded
            stream32 = rounded.astype(F32)
            normed[b, rows, :] = (stream32 * inverse_of(stream32)).astype(BF16)
        return carry

    lax.fori_loop(0, 4, settle, 0)
    factor = logit_scale / math.sqrt(width)
    for b in range(2):
        rows = normed[b]
        ex = jnp.exp(factor * times_t(unit, rows))
        expo[b] = ex
        dispatch32 = ex / jnp.sum(ex, axis=1, keepdims=True)
        spread32[b] = dispatch32
        natural[0, 64 * b : 64 * b + 64] = times(dispatch32.astype(BF16), rows).astype(BF16)
    pairs[0] = reorder(to_pairs, natural[0])

    def swap(kind):
        return (
            xy,
            lambda k: rows8(pairs, kind, k),
            lambda k: rows8(came, kind, k),
            s1.at[kind],
            r1.at[kind],
        )

    def keep(kind):
        return pltpu.make_async_copy(
            rows8(pairs, kind, xy), rows8(came, kind, xy), s1.at[kind, 0]
        )

    entered()
    keep(0).start()
    xy_start(*swap(0))
    for b in range(2):
        ex = expo[b]
        combine32 = ex / jnp.sum(ex, axis=0, keepdims=True)
        expo[b] = combine32
        natural[1, 64 * b : 64 * b + 64] = times(combine32.astype(BF16), cot[b]).astype(BF16)
    pairs[1] = reorder(to_pairs, natural[1])
    keep(1).start()
    xy_start(*swap(1))

    def there(kind, e, zz):
        return x.at[kind, e, zz, core]

    def send(kind, e, number, src, zz, device):
        return remote(
            src, there(kind, e, zz), s2.at[kind, e, number], r2.at[kind, e, number], device
        )

    c, m, f = cross(z), mate(z), far(z)

    def to_mate(kind, e):
        return send(kind, e, 0, blocks.at[kind, zh, e], z, at_z(m))

    def to_cross(kind, e):
        return send(kind, e, 1, blocks.at[kind, flip(zh), e], z, at_z(c))

    def on_mate(kind, e):
        return send(kind, e, 2, there(kind, e, c), c, at_z(m))

    def to_core(kind, e, number):
        if number == 3:
            return send(kind, e, 3, blocks.at[kind, zh, e], z, partner)
        zz = (c, m, f)[number - 4]
        return send(kind, e, number, there(kind, e, zz), zz, partner)

    def mine(kind, e):
        return pltpu.make_async_copy(
            blocks.at[kind, zh, e], there(kind, e, z), s2.at[kind, e, 7]
        )

    def spread(kind):
        keep(kind).wait()
        xy_wait(*swap(kind))
        ordered = reorder(to_blocks, came[kind])
        for i in range(2):
            for e in range(2):
                blocks[kind, i, e] = ordered[i * 64 + e * 32 : i * 64 + e * 32 + 32]
        for e in range(2):
            to_cross(kind, e).start()
            to_mate(kind, e).start()
            to_core(kind, e, 3).start()
            mine(kind, e).start()

    def relay(kind, e):
        to_cross(kind, e).wait_recv()
        on_mate(kind, e).start()
        to_core(kind, e, 4).start()
        to_mate(kind, e).wait_recv()
        to_core(kind, e, 5).start()

    def relay_last(kind, e):
        on_mate(kind, e).wait_recv()
        to_core(kind, e, 6).start()

    def arrived(kind, e):
        mine(kind, e).wait()
        for number in range(3, 7):
            to_core(kind, e, number).wait_recv()

    def sent(kind, e):
        to_mate(kind, e).wait_send()
        to_cross(kind, e).wait_send()
        on_mate(kind, e).wait_send()
        for number in range(3, 7):
            to_core(kind, e, number).wait_send()

    def rows_of(kind, e):
        return x[kind, e].reshape(256, width)

    cut = 512

    def up(e):
        rows = rows_of(0, e)
        for n in range(0, hidden, cut):
            value, rise = curve(times(rows, wi[e, :, n : n + cut]))
            act[e, :, n : n + cut] = value.astype(BF16)
            slope[e, :, n : n + cut] = rise

    def down(e):
        rows = act[e]
        for n in range(0, width, cut):
            part = times(rows, wo[e, :, n : n + cut]).astype(BF16)
            o[0, e, :, :, :, n : n + cut] = part.reshape(4, 2, 32, cut)

    def back_down(e):
        rows = rows_of(1, e)
        for n in range(0, hidden, cut):
            rise = times_t(rows, wo[e, n : n + cut, :])
            gpre[e, :, n : n + cut] = (rise * slope[e, :, n : n + cut]).astype(BF16)

    def back_up(e):
        rows = gpre[e]
        for n in range(0, width, cut):
            part = times_t(rows, wi[e, n : n + cut, :]).astype(BF16)
            o[1, e, :, :, :, n : n + cut] = part.reshape(4, 2, 32, cut)

    def home_core(kind, e):
        return remote(
            o.at[kind, e, :, flip(core)], halves.at[kind, e], sa.at[kind, e], ra.at[kind, e], partner
        )

    def home_mate(kind, e):
        return [
            remote(
                chip.at[kind, zz, e],
                paired.at[kind, i, e],
                sb.at[kind, e, i],
                rb.at[kind, e, i],
                at_z(m),
            )
            for i, zz in enumerate((f, m))
        ]

    def home_cross(kind, e):
        return remote(
            crossing.at[kind, e],
            blocks2.at[kind, zh, e],
            sb.at[kind, e, 2],
            rb.at[kind, e, 2],
            at_z(c),
        )

    def home_swap(kind):
        return (
            xy,
            lambda k: rows8(pairs2, kind, k),
            lambda k: rows8(came2, kind, k),
            sc.at[kind],
            rc.at[kind],
        )

    def home_keep(kind):
        return pltpu.make_async_copy(
            rows8(pairs2, kind, xy), rows8(came2, kind, xy), sc.at[kind, 0]
        )

    def chip_sum(kind, e):
        home_core(kind, e).wait()
        for zz in range(4):
            chip[kind, zz, e] = (
                o[kind, e, zz, core].astype(F32) + halves[kind, e, zz].astype(F32)
            ).astype(BF16)
        home_mate(kind, e)[0].start()

    def pass_on(kind, e):
        home_mate(kind, e)[0].wait_recv()
        crossing[kind, e] = (
            chip[kind, c, e].astype(F32) + paired[kind, 0, e].astype(F32)
        ).astype(BF16)
        home_cross(kind, e).start()

    def pair_sum(kind, e):
        home_mate(kind, e)[1].wait_recv()
        blocks2[kind, zh, e] = (
            chip[kind, z, e].astype(F32) + paired[kind, 1, e].astype(F32)
        ).astype(BF16)

    def home(kind):
        for e in range(2):
            home_cross(kind, e).wait_recv()
        rows = jnp.concatenate([blocks2[kind, i, e] for i in range(2) for e in range(2)], axis=0)
        pairs2[kind] = reorder(from_blocks, rows)
        home_keep(kind).start()
        xy_start(*home_swap(kind))

    def landed(kind):
        home_keep(kind).wait()
        xy_wait(*home_swap(kind))
        out[kind] = reorder(from_pairs, came2[kind])

    spread(0)
    spread(1)
    relay(0, 0)
    relay(0, 1)
    relay_last(0, 0)
    relay(1, 0)
    relay_last(0, 1)
    relay(1, 1)
    load_in.wait()
    load_out.wait()
    arrived(0, 0)
    up(0)
    relay_last(1, 0)
    arrived(0, 1)
    up(1)
    relay_last(1, 1)
    for e in range(2):
        down(e)
        home_core(0, e).start()
    arrived(1, 0)
    back_down(0)
    back_up(0)
    home_core(1, 0).start()
    chip_sum(0, 0)
    chip_sum(0, 1)
    arrived(1, 1)
    back_down(1)
    back_up(1)
    home_core(1, 1).start()
    chip_sum(1, 0)
    pass_on(0, 0)
    pass_on(0, 1)
    chip_sum(1, 1)
    for e in range(2):
        home_mate(0, e)[1].start()
    for e in range(2):
        home_mate(1, e)[1].start()
    pass_on(1, 0)
    pass_on(1, 1)
    for e in range(2):
        pair_sum(0, e)
    home(0)
    for e in range(2):
        pair_sum(1, e)
    home(1)
    landed(0)
    for b in range(2):
        combine32 = expo[b]
        grad_combine = times_t(out[0, 64 * b : 64 * b + 64], cot[b])
        pulled[b] = combine32 * (
            grad_combine - jnp.sum(combine32 * grad_combine, axis=0, keepdims=True)
        )
    landed(1)
    for kind in range(2):
        for e in range(2):
            sent(kind, e)
            for copy in home_mate(kind, e):
                copy.wait_send()
            home_cross(kind, e).wait_send()


def sum_kernel(
    back, stream, normed, spread32, pulled, whole, ctx, cot, slots,
    gctx, gres, out, u_out,
    slots_here, gn, unit_part,
    gs, ga, mine, gq, gb, gh, gc, gt, gf, gv, gall,
    ua, uw, uc, ut, uz, uv, uall, uother,
    sw, sg, rg, su, ru, s1, r1, s2, r2, s3, r3, s4, r4,
):
    z, core, xy = place()
    zl = lax.rem(z, 2)
    partner = at_core(flip(core))
    ring = [at_z(lax.rem(z + d, 4)) for d in range(1, 4)]
    width = stream.shape[-1]
    quarter = width // 4
    half = quarter // 2
    chunk = quarter // 16
    wide = width // 4
    cut = width // PIECES
    factor = logit_scale / math.sqrt(width)
    load_slots = pltpu.make_async_copy(slots, slots_here, sw.at[0])
    load_slots.start()
    load_slots.wait()
    unit32, norm = unit_of(slots_here)
    unit = unit32.astype(BF16)
    for b in range(2):
        dispatch32 = spread32[b]
        grad_in = back[1, 64 * b : 64 * b + 64]
        grad_dispatch = times_t(grad_in, normed[b])
        grad_logits = pulled[b] + dispatch32 * (
            grad_dispatch - jnp.sum(dispatch32 * grad_dispatch, axis=1, keepdims=True)
        )
        grad_logits = grad_logits.astype(BF16)
        part = times(grad_logits, normed[b])
        for i in range(2):
            rows = part[32 * i : 32 * i + 32]
            unit_part[i] = rows if b == 0 else unit_part[i] + rows
        gn[b] = t_times(dispatch32.astype(BF16), grad_in) + factor * t_times(grad_logits, unit)
    u_core = remote(unit_part.at[flip(core)], ua, su.at[0], ru.at[0], partner)
    u_core.start()

    def settle(i, carry):
        for b in range(2):
            rows = pl.ds(pl.multiple_of(i * 64, 64), 64)
            stream32 = stream[b, rows, :].astype(F32)
            inverse = inverse_of(stream32)
            normed32 = stream32 * inverse
            grad = gn[b, rows, :]
            pull = jnp.mean(normed32 * grad, axis=1, keepdims=True)
            gres[b, rows, :] = (
                cot[b, rows, :].astype(F32) + inverse * (grad - normed32 * pull)
            ).astype(BF16)
        return carry

    lax.fori_loop(0, 4, settle, 0)


    def proj(block, h):
        left = ctx[:, :, pl.ds(pl.multiple_of(block * quarter, quarter), quarter)]
        right = gres[:, :, cut * h : cut * h + cut]
        return t_times(left.reshape(512, quarter), right.reshape(512, cut))

    def g_core(h, i):
        return remote(gs.at[h, i], ga.at[h, i], sg.at[h, i], rg.at[h, i], partner)

    def g_mate(h):
        return remote(
            gq.at[h, pl.ds(0, half)], gb.at[h, pl.ds(0, half)], sg.at[h, 2], rg.at[h, 2], at_z(mate(z))
        )

    def g_cross(h):
        return remote(
            gq.at[h, pl.ds(half, half)],
            gb.at[h, pl.ds(half, half)],
            sg.at[h, 3],
            rg.at[h, 3],
            at_z(cross(z)),
        )

    def g_swap(h):
        return (
            xy,
            lambda k: gh.at[h, pl.ds(pl.multiple_of(chunk * k, chunk), chunk)],
            lambda k: gc.at[h, k],
            s2.at[h],
            r2.at[h],
        )

    def g_keep(h):
        return pltpu.make_async_copy(g_swap(h)[1](xy), gc.at[h, xy], s2.at[h, 0])

    def g_far(h):
        return remote(gt.at[h], gf.at[h], sg.at[h, 4], rg.at[h, 4], at_z(far(z)))

    def g_back(h):
        return (xy, lambda k: gv.at[h], lambda k: gall.at[h, k], s4.at[h], r4.at[h])

    def g_stay(h):
        return pltpu.make_async_copy(gv.at[h], gall.at[h, xy], s4.at[h, 0])

    blocks = (2 * flip(zl), 2 * zl)
    u_swap = (xy, lambda k: uw.at[k], lambda k: uc.at[k], s1, r1)
    u_keep = pltpu.make_async_copy(uw.at[xy], uc.at[xy], s1.at[0])

    pieces = range(PIECES)
    for h in pieces:
        gs[h, 0] = proj(blocks[0] + flip(core), h).astype(BF16)
        g_core(h, 0).start()
    u_core.wait()
    for i in range(4):
        for j in range(4):
            rows, columns = slice(8 * i, 8 * i + 8), slice(wide * j, wide * j + wide)
            uw[4 * i + j] = unit_part[core, rows, columns] + ua[rows, columns]
    u_keep.start()
    xy_start(*u_swap)
    for h in pieces:
        part = proj(blocks[0] + core, h)
        g_core(h, 0).wait()
        gq[h] = (part + ga[h, 0].astype(F32)).astype(BF16)
        g_mate(h).start()
        g_cross(h).start()
    for h in pieces:
        gs[h, 1] = proj(blocks[1] + flip(core), h).astype(BF16)
        g_core(h, 1).start()
    for h in pieces:
        mine[h] = proj(blocks[1] + core, h)

    u_ring = [remote(ut, uz.at[z], su.at[d + 1], ru.at[d + 1], ring[d]) for d in range(3)]
    u_mine = pltpu.make_async_copy(ut, uz.at[z], su.at[4])
    u_back = (xy, lambda k: uv, lambda k: uall.at[k], s3, r3)
    u_stay = pltpu.make_async_copy(uv, uall.at[xy], s3.at[0])
    u_other = remote(uall, uother, su.at[5], ru.at[5], partner)

    def u_first():
        u_keep.wait()
        xy_wait(*u_swap)
        ut[...] = jnp.sum(uc[...], axis=0)
        u_mine.start()
        for copy in u_ring:
            copy.start()

    def u_second():
        u_mine.wait()
        for copy in u_ring:
            copy.wait()
        uv[...] = jnp.sum(uz[...], axis=0)
        u_stay.start()
        xy_start(*u_back)

    def u_third():
        u_stay.wait()
        xy_wait(*u_back)
        u_other.start()

    def chip_rows(h):
        g_core(h, 1).wait()
        g_mate(h).wait()
        g_cross(h).wait()
        gh[h] = (mine[h] + ga[h, 1].astype(F32) + gb[h].astype(F32)).astype(BF16)
        g_keep(h).start()
        xy_start(*g_swap(h))

    def plane_sum(h):
        g_keep(h).wait()
        xy_wait(*g_swap(h))
        total = gc[h, 0].astype(F32)
        for k in range(1, 16):
            total = total + gc[h, k].astype(F32)
        gt[h] = total.astype(BF16)
        g_far(h).start()

    def far_sum(h):
        g_far(h).wait()
        gv[h] = (gt[h].astype(F32) + gf[h].astype(F32)).astype(BF16)
        g_stay(h).start()
        xy_start(*g_back(h))

    def finish(h):
        g_stay(h).wait()
        xy_wait(*g_back(h))
        for k in range(16):
            out[chunk * k : chunk * k + chunk, cut * h : cut * h + cut] = gall[h, k].astype(F32)

    def grad_context(h):
        for b in range(2):
            columns = slice(cut * h, cut * h + cut)
            gctx[b, :, columns] = times_t(gres[b], whole[columns, :]).astype(BF16)

    for h in pieces:
        chip_rows(h)
        if h == 0:
            u_first()
        grad_context(h)
    u_second()
    for h in pieces:
        plane_sum(h)
        if h:
            far_sum(h - 1)
    far_sum(PIECES - 1)
    u_third()
    u_other.wait()
    for i in range(4):
        for j in range(4):
            columns = slice(wide * j, wide * j + wide)
            rows = slice(8 * i, 8 * i + 8)
            unit_part[core, rows, columns] = uall[4 * i + j]
            unit_part[flip(core), rows, columns] = uother[4 * i + j]
    grad_unit = factor * unit_part[...].reshape(64, width)
    u_out[...] = (
        grad_unit - unit32 * jnp.sum(unit32 * grad_unit, axis=1, keepdims=True)
    ) / norm
    for h in pieces:
        finish(h)


def layer_kernel(ctx, cot, whole, total, slots, win, wout, *refs):
    x, act, gpre, gctx, gres, gproj, gslots, back, stream, normed, spread32, pulled = refs[:12]
    first, second = refs[12 : 12 + FIRST], refs[12 + FIRST :]
    expert_kernel(
        ctx, cot, whole, total, slots, win, wout,
        back, stream, normed, spread32, pulled, x, act, gpre, *first,
    )
    sum_kernel(
        back, stream, normed, spread32, pulled, whole, ctx, cot, slots,
        gctx, gres, gproj, gslots, *second,
    )


def layer(ctx, cot, whole, total, slots, expert_in, expert_out):
    width = ctx.shape[-1]
    hidden = expert_in.shape[-1]
    rows = width // 4
    chunk = rows // 16
    wide = width // 4
    cut = width // PIECES
    dma = pltpu.SemaphoreType.DMA
    here = pl.BlockSpec(memory_space=VMEM)
    afar = pl.BlockSpec(memory_space=pltpu.HBM)
    first = [
        VMEM(slots.shape, BF16),
        VMEM((2, 128, width), BF16),
        VMEM((2, 64, 256), F32),
        VMEM((2, 128, width), BF16),
        VMEM((2, 128, width), BF16),
        VMEM((2, 2, 2, 32, width), BF16),
        VMEM(expert_in.shape, BF16),
        VMEM(expert_out.shape, BF16),
        VMEM((2, 256, hidden), F32),
        VMEM((2, 2, 4, 2, 32, width), BF16),
        VMEM((2, 2, 4, 32, width), BF16),
        VMEM((2, 4, 2, 32, width), BF16),
        VMEM((2, 2, 2, 32, width), BF16),
        VMEM((2, 2, 32, width), BF16),
        VMEM((2, 2, 2, 32, width), BF16),
        VMEM((2, 128, width), BF16),
        VMEM((2, 128, width), BF16),
        dma((2, 16)),
        dma((2, 16)),
        dma((2, 2, 8)),
        dma((2, 2, 8)),
        dma((2, 2)),
        dma((2, 2)),
        dma((2, 2, 3)),
        dma((2, 2, 3)),
        dma((2, 16)),
        dma((2, 16)),
        dma((3,)),
    ]
    second = [
        VMEM(slots.shape, BF16),
        VMEM(ctx.shape, F32),
        VMEM((2, 32, width), F32),
        VMEM((PIECES, 2, rows, cut), BF16),
        VMEM((PIECES, 2, rows, cut), BF16),
        VMEM((PIECES, rows, cut), F32),
        VMEM((PIECES, rows, cut), BF16),
        VMEM((PIECES, rows, cut), BF16),
        VMEM((PIECES, rows, cut), BF16),
        VMEM((PIECES, 16, chunk, cut), BF16),
        VMEM((PIECES, chunk, cut), BF16),
        VMEM((PIECES, chunk, cut), BF16),
        VMEM((PIECES, chunk, cut), BF16),
        VMEM((PIECES, 16, chunk, cut), BF16),
        VMEM((32, width), F32),
        VMEM((16, 8, wide), F32),
        VMEM((16, 8, wide), F32),
        VMEM((8, wide), F32),
        VMEM((4, 8, wide), F32),
        VMEM((8, wide), F32),
        VMEM((16, 8, wide), F32),
        VMEM((16, 8, wide), F32),
        dma((1,)),
        dma((PIECES, 5)),
        dma((PIECES, 5)),
        dma((6,)),
        dma((6,)),
        dma((16,)),
        dma((16,)),
        dma((PIECES, 16)),
        dma((PIECES, 16)),
        dma((16,)),
        dma((16,)),
        dma((PIECES, 16)),
        dma((PIECES, 16)),
    ]
    assert len(first) == FIRST
    return pl.pallas_call(
        layer_kernel,
        out_shape=(
            jax.ShapeDtypeStruct((2, 2, 4, 2, 32, width), BF16),
            jax.ShapeDtypeStruct((2, 256, hidden), BF16),
            jax.ShapeDtypeStruct((2, 256, hidden), BF16),
            jax.ShapeDtypeStruct(ctx.shape, BF16),
            jax.ShapeDtypeStruct(ctx.shape, BF16),
            jax.ShapeDtypeStruct((rows, width), F32),
            jax.ShapeDtypeStruct((64, width), F32),
        ),
        in_specs=[here] * 4 + [afar] * 3,
        out_specs=(here,) * 7,
        scratch_shapes=[
            VMEM((2, 128, width), BF16),
            VMEM(ctx.shape, BF16),
            VMEM(ctx.shape, BF16),
            VMEM((2, 64, 256), F32),
            VMEM((2, 64, 256), F32),
            *first,
            *second,
        ],
        compiler_params=params(2, 40 << 20),
        name="layer",
    )(ctx, cot, whole, total, slots, expert_in, expert_out)


def result_kernel(
    x, act, gpre, gctx, gres, gproj, gslots,
    to_ctx, to_res, to_proj, to_slots, to_in, to_out,
    gi, go, sem, wsem,
):
    width = x.shape[-1]
    cut = width // 2
    ready = [
        pltpu.make_async_copy(src, dst, sem.at[i])
        for i, (src, dst) in enumerate(
            ((gctx, to_ctx), (gres, to_res), (gproj, to_proj), (gslots, to_slots))
        )
    ]
    for copy in ready:
        copy.start()
    copies = []
    for e in range(2):
        first, second = (x[kind, e].reshape(256, width) for kind in range(2))
        for i in range(2):
            rows = pl.ds(cut * i, cut)
            go[e, rows, :] = t_times(act[e, :, rows], second).astype(BF16)
            copies.append(
                pltpu.make_async_copy(go.at[e, rows], to_out.at[e, rows], wsem.at[0, e, i])
            )
            copies[-1].start()
            gi[e, rows, :] = t_times(first[:, cut * i : cut * i + cut], gpre[e]).astype(BF16)
            copies.append(
                pltpu.make_async_copy(gi.at[e, rows], to_in.at[e, rows], wsem.at[1, e, i])
            )
            copies[-1].start()
    for copy in ready + copies:
        copy.wait()


def results(x, act, gpre, gctx, gres, gproj, gslots):
    width = x.shape[-1]
    hidden = act.shape[-1]
    dma = pltpu.SemaphoreType.DMA
    afar = pl.BlockSpec(memory_space=pltpu.HBM)
    shapes = (
        jax.ShapeDtypeStruct((2, width, hidden), BF16),
        jax.ShapeDtypeStruct((2, hidden, width), BF16),
    )
    return pl.pallas_call(
        result_kernel,
        out_shape=tuple(
            jax.ShapeDtypeStruct(a.shape, a.dtype) for a in (gctx, gres, gproj, gslots)
        )
        + shapes,
        in_specs=[pl.BlockSpec(memory_space=VMEM)] * 7,
        out_specs=(afar,) * 6,
        scratch_shapes=[
            VMEM(shapes[0].shape, BF16),
            VMEM(shapes[1].shape, BF16),
            dma((4,)),
            dma((2, 2, 2)),
        ],
        compiler_params=pltpu.CompilerParams(vmem_limit_bytes=24 << 20),
        name="results",
    )(x, act, gpre, gctx, gres, gproj, gslots)


def shards(context, residual, cotangent, proj_weight, slot_params, expert_in, expert_out):
    slots = slot_params.T
    context, residual, cotangent, proj_weight, slots, expert_in, expert_out = (
        pltpu.with_memory_space_constraint(a, pltpu.HBM)
        for a in (context, residual, cotangent, proj_weight, slots, expert_in, expert_out)
    )
    whole, total, ctx, cot = project(context, residual, cotangent, proj_weight)
    made = layer(ctx, cot, whole, total, slots, expert_in, expert_out)
    grad_context, grad_residual, grad_proj, grad_slots, grad_in, grad_out = results(*made)
    return grad_context, grad_residual, grad_proj, grad_slots.T, grad_in, grad_out


def solution(mesh):
    torus = Mesh(mesh.devices.reshape(2, 2, 4, 4, 2), AXES)
    placed = (
        P(IMG_EXP, None, None),
        P(IMG_EXP, None, None),
        P(IMG_EXP, None, None),
        P(IMG, None),
        P(),
        P(EXP, None, IMG),
        P(EXP, IMG, None),
    )
    return jax.shard_map(
        shards,
        mesh=torus,
        in_specs=placed,
        out_specs=(
            P(IMG_EXP, None, None),
            P(IMG_EXP, None, None),
            P(IMG, None),
            P(),
            P(EXP, None, IMG),
            P(EXP, IMG, None),
        ),
        check_vma=False,
    )
```
